32 devices in a mesh: img: 4 (over z), seq: 4 (over x, core), head: 2 (over y).
Axes of the slice: x: 2, y: 2, z: 4, core: 2. Of those that a mesh axis runs over, the one named last changes fastest.
Arguments:
- self_qkv: bfloat16 [4, 1024, 3072], P('img', ('seq', 'head')), may hold values from -12 to 12
- cross_query: bfloat16 [4, 1024, 1024], P('img', ('seq', 'head')), may hold values from -12 to 12
- thermal_kv: bfloat16 [4, 8, 256, 2048], P('img', ('seq', 'head')), may hold values from -12 to 12
- owners: int32 [4], P('img'), may hold values from 0 to 7
- grad_out: bfloat16 [4, 1024, 1024], P('img', ('seq', 'head')), may hold values from -6 to 6
Outputs:
- combined: bfloat16 [4, 1024, 1024], P('img', ('seq', 'head'))
- grad_qkv: bfloat16 [4, 1024, 3072], P('img', ('seq', 'head'))
- grad_cross_query: bfloat16 [4, 1024, 1024], P('img', ('seq', 'head'))
- grad_thermal: bfloat16 [4, 256, 2048], P('img', ('seq', 'head'))
The draws below stay inside these ranges and needn't reach their ends.
All inputs are finite; a program needn't handle non-finite values.
Results may differ from the reference program's by a relative error of at most 0.012.
The reference program's roundings to bfloat16 on the way count: a program that leaves them out, or rounds other values in their place, can miss the bound.
Values may be sent and summed in bfloat16 or wider, within the bound.
No kernel may reach another device: no remote copies, remote signals or barrier semaphores. Data moves between devices by JAX's collectives and lax.ppermute only.
A program may use at most 128 MiB of HBM per device.

```python
import math
import jax
import jax.numpy as jnp
from jax import lax

HEADS = 16
HD = 64
D = 1024
M = 256
L = 1024
GROUP = 8
IMAGES = 4


def base_values(key, shape):
    return jnp.clip(jax.random.normal(key, shape, jnp.float32), -6.0, 6.0)


def draw_self_qkv(key, part):
    values = base_values(jax.random.fold_in(key, 1), (IMAGES, L, 3 * D))
    return values.astype(jnp.bfloat16)


def draw_cross_query(key, part):
    values = base_values(jax.random.fold_in(key, 2), (IMAGES, L, D))
    return values.astype(jnp.bfloat16)


def draw_thermal_kv(key, part):
    values = base_values(jax.random.fold_in(key, 3), (IMAGES, GROUP, M, 2 * D))
    return values.astype(jnp.bfloat16)


def plant(drawn, stream_key, low, largest):
    extent = drawn.shape
    index_at = [jax.random.randint(jax.random.fold_in(stream_key, axis), (), 0, extent[axis]) for axis in range(len(extent))]
    drawn = drawn.at[tuple(index_at)].set(low)
    longest = extent.index(max(extent))
    index_at[longest] = (index_at[longest] + 1) % extent[longest]
    return drawn.at[tuple(index_at)].set(largest)


def block_scale(key, dims, cuts, smallest, high):
    level = 1.0
    for dim, blocks in cuts:
        heights = jax.random.uniform(jax.random.fold_in(jax.random.fold_in(key, 6), dim), (blocks,), jnp.float32, smallest / len(cuts), high / len(cuts))
        level = level * jnp.repeat(jnp.exp(heights), dims[dim] // blocks).reshape((-1,) + (1,) * (len(dims) - 1 - dim))
    return level


def gaussian(own_key, shape, deviation, bound, shards=(), kind=jnp.bfloat16):
    result = deviation * jax.random.normal(own_key, shape, jnp.float32)
    if shards:
        result = result * block_scale(own_key, shape, shards, -0.22, 0.18)
    return jnp.clip(result, -bound, bound).astype(kind)


def setup_inputs(seed: int = 0) -> dict:
    key_of = jax.random.split(jax.random.key(seed), 6)
    return {
        "self_qkv": draw_self_qkv(jax.random.fold_in(key_of[5], 71), 0),
        "cross_query": draw_cross_query(jax.random.fold_in(key_of[5], 71), 0),
        "thermal_kv": draw_thermal_kv(jax.random.fold_in(key_of[5], 71), 0),
        "owners": plant(jax.random.randint(key_of[3], (IMAGES,), 0, GROUP), jax.random.fold_in(key_of[3], 1), 0, GROUP - 1).astype(jnp.int32),
        "grad_out": gaussian(key_of[4], (IMAGES, L, D), 1.0, 6.0, ((0, 4), (1, 8))),
    }


def log_total(scores):
    row_max = lax.optimization_barrier(jnp.max(scores, axis=-1, keepdims=True))
    return row_max + jnp.log(lax.optimization_barrier(jnp.sum(jnp.exp(scores - row_max), axis=-1, keepdims=True)))

def split_heads(matrix):
    return matrix.reshape(matrix.shape[0], HEADS, HD).transpose(1, 0, 2)

def join_heads(stacked):
    return stacked.transpose(1, 0, 2).reshape(stacked.shape[1], HEADS * HD)

def forward_head(packed):
    query, keys, values = packed
    score_scale = 1.0 / math.sqrt(HD)
    scores = jnp.dot(query, keys.T, preferred_element_type=jnp.float32) * score_scale
    log_sum = log_total(scores)
    probs = jnp.exp(scores - log_sum).astype(jnp.bfloat16)
    return (jnp.dot(probs, values, preferred_element_type=jnp.float32), log_sum)

def backward_head(packed):
    query, keys, values, upstream, log_sum = packed
    score_scale = 1.0 / math.sqrt(HD)
    scores = jnp.dot(query, keys.T, preferred_element_type=jnp.float32) * score_scale
    probs = jnp.exp(scores - log_sum).astype(jnp.bfloat16)
    dprobs = jnp.dot(upstream, values.T, preferred_element_type=jnp.float32)
    delta = lax.optimization_barrier(jnp.sum(probs.astype(jnp.float32) * dprobs, axis=-1, keepdims=True))
    dscores = (probs.astype(jnp.float32) * (dprobs - delta) * score_scale).astype(jnp.bfloat16)
    query_grad = jnp.dot(dscores, keys, preferred_element_type=jnp.float32)
    key_grad = jnp.dot(dscores.T, query, preferred_element_type=jnp.float32)
    value_grad = jnp.dot(probs.T, upstream, preferred_element_type=jnp.float32)
    return (query_grad, key_grad, value_grad)

def one_image(packed):
    projections, cross_term, thermal_all, owner_index, upstream = packed
    model_width = HEADS * HD
    query_heads = split_heads(projections[:, :model_width])
    key_heads = split_heads(projections[:, model_width:2 * model_width])
    value_heads = split_heads(projections[:, 2 * model_width:])
    self_out, self_lse = lax.map(forward_head, (query_heads, key_heads, value_heads))
    attended = join_heads(self_out).astype(jnp.bfloat16)
    cross_in = (attended.astype(jnp.float32) + cross_term.astype(jnp.float32)).astype(jnp.bfloat16)
    thermal = lax.dynamic_index_in_dim(thermal_all, owner_index, 0, keepdims=False)
    thermal_keys = split_heads(thermal[:, :model_width])
    thermal_values = split_heads(thermal[:, model_width:])
    cross_heads = split_heads(cross_in)
    cross_out, cross_lse = lax.map(forward_head, (cross_heads, thermal_keys, thermal_values))
    combined = (attended.astype(jnp.float32) + join_heads(cross_out)).astype(jnp.bfloat16)
    upstream_heads = split_heads(upstream)
    cross_dq, cross_dk, cross_dv = lax.map(backward_head, (cross_heads, thermal_keys, thermal_values, upstream_heads, cross_lse))
    cross_grad = join_heads(cross_dq)
    grad_cross = cross_grad.astype(jnp.bfloat16)
    grad_thermal = jnp.concatenate([join_heads(cross_dk), join_heads(cross_dv)], axis=1).astype(jnp.bfloat16)
    attended_grad = (upstream.astype(jnp.float32) + cross_grad).astype(jnp.bfloat16)
    self_dq, self_dk, self_dv = lax.map(backward_head, (query_heads, key_heads, value_heads, split_heads(attended_grad), self_lse))
    grad_qkv = jnp.concatenate([join_heads(self_dq), join_heads(self_dk), join_heads(self_dv)], axis=1).astype(jnp.bfloat16)
    return (combined, grad_qkv, grad_cross, grad_thermal)

def reference(self_qkv, cross_query, thermal_kv, owners, grad_out):
    results = lax.map(one_image, (self_qkv, cross_query, thermal_kv, owners.astype(jnp.int32), grad_out))
    return (results[0], results[1], results[2], results[3])
```

```python
import functools
import math

import jax
import jax.numpy as jnp
from jax import lax
from jax.experimental import pallas as pl
from jax.experimental.pallas import tpu as pltpu
from jax.sharding import PartitionSpec as P
BF=jnp.bfloat16; F=jnp.float32
HD=64
VM=pl.BlockSpec(memory_space=pltpu.VMEM)
NT=(((1,),(1,)),((),()))
def dot(a,b): return jnp.dot(a,b,preferred_element_type=F)
def dot_nt(a,b): return lax.dot_general(a,b,NT,preferred_element_type=F)
def tr(x): return x.T
def head_only(x,h):
    if x.shape[-1]==HD: return x
    lane=lax.broadcasted_iota(jnp.int32,x.shape,1)
    return jnp.where((lane>=h*HD)&(lane<(h+1)*HD),x,jnp.zeros_like(x))
def softmax_t(sT):
    c=1.0/math.sqrt(HD)
    m=jnp.max(sT,axis=0,keepdims=True)
    e=jnp.exp((sT-m)*c)
    l=jnp.sum(e,axis=0,keepdims=True)
    return (e*(1.0/l)).astype(BF)
def self_fwd_kernel(qkv_ref,pT_ref,oT_ref,vT_ref,*,QB):
    G,R,W3=qkv_ref.shape; W=W3//3; L=G*R; Hl=W//HD
    nb=QB//R
    k=qkv_ref[:,:,W:2*W].reshape(L,W)
    vT_ref[...]=tr(qkv_ref[:,:,2*W:].reshape(L,W))
    for h in range(Hl):
        for b in range(L//QB):
            q=qkv_ref[b*nb:(b+1)*nb,:,:W].reshape(QB,W)
            p=softmax_t(dot_nt(k,head_only(q,h)))
            pT_ref[h,:,b*QB:(b+1)*QB]=p
            oT_ref[h*HD:(h+1)*HD,b*QB:(b+1)*QB]=dot(vT_ref[h*HD:(h+1)*HD,:],p)
def self_fwd(qkv,QB=256):
    G,R,W3=qkv.shape; W=W3//3; L=G*R; Hl=W//HD
    return pl.pallas_call(functools.partial(self_fwd_kernel,QB=QB),
        out_shape=(jax.ShapeDtypeStruct((Hl,L,L),BF),jax.ShapeDtypeStruct((W,L),F)),
        in_specs=[VM],out_specs=(VM,VM),scratch_shapes=[pltpu.VMEM((W,L),BF)],name="self_fwd",
        compiler_params=pltpu.CompilerParams(vmem_limit_bytes=56<<20))(qkv)
def self_bwd_kernel(qkv_ref,pT_ref,oT_ref,ag_ref,out_ref,kT_ref,dk_ref,dv_ref,*,QB):
    G,R,W3=qkv_ref.shape; W=W3//3; L=G*R; Hl=W//HD
    nb=QB//R; c=1.0/math.sqrt(HD)
    v=qkv_ref[:,:,2*W:].reshape(L,W)
    kT_ref[...]=tr(qkv_ref[:,:,W:2*W].reshape(L,W))
    for b in range(L//QB):
        ag=ag_ref[b*nb:(b+1)*nb].reshape(QB,W)
        q=qkv_ref[b*nb:(b+1)*nb,:,:W].reshape(QB,W)
        prod=tr(ag).astype(F)*oT_ref[:,b*QB:(b+1)*QB]
        dqs=[]
        for h in range(Hl):
            delta=jnp.sum(prod[h*HD:(h+1)*HD],axis=0,keepdims=True)
            agh=head_only(ag,h)
            p=pT_ref[h,:,b*QB:(b+1)*QB]
            dv=dot(p,agh)
            dp=dot_nt(v,agh)
            ds=(p.astype(F)*(dp-delta)).astype(BF)
            dk=dot(ds,head_only(q,h))
            dqs.append(dot(kT_ref[h*HD:(h+1)*HD,:],ds))
            if b==0 and h==0:
                dk_ref[...]=dk; dv_ref[...]=dv
            else:
                dk_ref[...]+=dk; dv_ref[...]+=dv
        dqT=jnp.concatenate(dqs,axis=0)*c
        out_ref[b*nb:(b+1)*nb,:,:W]=tr(dqT).astype(BF).reshape(nb,R,W)
    out_ref[:,:,W:2*W]=(dk_ref[...]*c).astype(BF).reshape(G,R,W)
    out_ref[:,:,2*W:]=dv_ref[...].astype(BF).reshape(G,R,W)
def self_bwd(qkv,pT,oT,ag,QB=256):
    G,R,W3=qkv.shape; W=W3//3; L=G*R
    return pl.pallas_call(functools.partial(self_bwd_kernel,QB=QB),
        out_shape=jax.ShapeDtypeStruct(qkv.shape,BF),
        in_specs=[VM]*4,out_specs=VM,scratch_shapes=[pltpu.VMEM((W,L),BF),pltpu.VMEM((L,W),F),pltpu.VMEM((L,W),F)],name="self_bwd",
        compiler_params=pltpu.CompilerParams(vmem_limit_bytes=56<<20))(qkv,pT,oT,ag)
def cross_kernel(idx_ref,oT_ref,cg_ref,out_ref,ag_ref,*,QB):
    G,RM,W2=cg_ref.shape; W=W2//2; L=oT_ref.shape[1]; R=L//G; M2=RM-R; M=2*M2; Hl=W//HD
    nb=QB//R; c=1.0/math.sqrt(HD)
    t0=cg_ref[idx_ref[0],R:,:]; t1=cg_ref[idx_ref[1],R:,:]
    t=jnp.concatenate([t0,t1],axis=0)
    tk=t[:,:W]; tv=t[:,W:]
    tkT=tr(tk); tvT=tr(tv)
    dtk=None; dtv=None
    for b in range(L//QB):
        at=tr(oT_ref[:,b*QB:(b+1)*QB]).astype(BF)
        cq=cg_ref[b*nb:(b+1)*nb,:R,:W].reshape(QB,W)
        go=cg_ref[b*nb:(b+1)*nb,:R,W:].reshape(QB,W)
        goT=tr(go).astype(F)
        x=(at.astype(F)+cq.astype(F)).astype(BF)
        mixs=[];dqs=[]
        for h in range(Hl):
            xh=head_only(x,h); gh=head_only(go,h)
            p=softmax_t(dot_nt(tk,xh))
            mix=dot(tvT[h*HD:(h+1)*HD],p)
            delta=jnp.sum(goT[h*HD:(h+1)*HD]*mix,axis=0,keepdims=True)
            dp=dot_nt(tv,gh)
            ds=(p.astype(F)*(dp-delta)).astype(BF)
            dqs.append(dot(tkT[h*HD:(h+1)*HD],ds))
            mixs.append(mix)
            a=dot(ds,xh); v=dot(p,gh)
            dtk=a if dtk is None else dtk+a
            dtv=v if dtv is None else dtv+v
        mix=tr(jnp.concatenate(mixs,axis=0)); dq=tr(jnp.concatenate(dqs,axis=0))*c
        out_ref[b*nb:(b+1)*nb,:R,:W]=(at.astype(F)+mix).astype(BF).reshape(nb,R,W)
        out_ref[b*nb:(b+1)*nb,:R,W:]=dq.astype(BF).reshape(nb,R,W)
        ag_ref[b*nb:(b+1)*nb]=(go.astype(F)+dq).astype(BF).reshape(nb,R,W)
    MR=M//G
    out_ref[:,R:,:W]=(dtk*c).astype(BF).reshape(G,MR,W)
    out_ref[:,R:,W:]=dtv.astype(BF).reshape(G,MR,W)
def cross(idx,oT,cg,R,QB=256):
    G,RM,W2=cg.shape; W=W2//2; L=oT.shape[1]; M=2*(RM-R)
    return pl.pallas_call(functools.partial(cross_kernel,QB=QB),
        out_shape=(jax.ShapeDtypeStruct((G,R+M//G,2*W),BF),jax.ShapeDtypeStruct((G,R,W),BF)),
        in_specs=[pl.BlockSpec(memory_space=pltpu.SMEM),VM,VM],out_specs=(VM,VM),name="cross",
        compiler_params=pltpu.CompilerParams(vmem_limit_bytes=56<<20))(idx,oT,cg)


HEADS = 16
GROUP = ("seq", "head")


def pack_qkv_kernel(x_ref, out_ref):
    G, R, W3 = out_ref.shape
    W = W3 // 3
    for j in range(G):
        for t in range(3):
            out_ref[j, :, t * W : (t + 1) * W] = x_ref[:, (t * G + j) * W : (t * G + j + 1) * W]


def pack_qkv(x, G):
    R, D3 = x.shape
    return pl.pallas_call(
        pack_qkv_kernel,
        out_shape=jax.ShapeDtypeStruct((G, R, D3 // G), BF),
        in_specs=[VM],
        out_specs=VM,
        name="pack_qkv",
    )(x)


def pack_rest_kernel(pick_ref, cq_ref, go_ref, t_ref, got_ref, out_ref):
    G, RM, W2 = out_ref.shape
    W = W2 // 2
    R = cq_ref.shape[0]
    half = got_ref.shape[0]
    start = pl.multiple_of(pick_ref[0] * half, half)
    own = t_ref[pl.ds(start, half), :]
    kept = jnp.where(pick_ref[1] == 1, own, got_ref[...])
    for j in range(G):
        out_ref[j, :R, :W] = cq_ref[:, j * W : (j + 1) * W]
        out_ref[j, :R, W:] = go_ref[:, j * W : (j + 1) * W]
        out_ref[j, R:, :W] = kept[:, j * W : (j + 1) * W]
        out_ref[j, R:, W:] = kept[:, (G + j) * W : (G + j + 1) * W]


def pack_rest(pick, cq, go, t, got, G):
    R, D = cq.shape
    return pl.pallas_call(
        pack_rest_kernel,
        out_shape=jax.ShapeDtypeStruct((G, R + got.shape[0], 2 * D // G), BF),
        in_specs=[pl.BlockSpec(memory_space=pltpu.SMEM), VM, VM, VM, VM],
        out_specs=VM,
        name="pack_rest",
    )(pick, cq, go, t, got)


def unpack_cross_kernel(x_ref, comb_ref, dcq_ref, dt_ref):
    G, RM, W2 = x_ref.shape
    W = W2 // 2
    R = comb_ref.shape[0]
    for j in range(G):
        comb_ref[:, j * W : (j + 1) * W] = x_ref[j, :R, :W]
        dcq_ref[:, j * W : (j + 1) * W] = x_ref[j, :R, W:]
        dt_ref[:, j * W : (j + 1) * W] = x_ref[j, R:, :W]
        dt_ref[:, (G + j) * W : (G + j + 1) * W] = x_ref[j, R:, W:]


def unpack_cross(x, R):
    G, RM, W2 = x.shape
    D = G * W2 // 2
    return pl.pallas_call(
        unpack_cross_kernel,
        out_shape=(
            jax.ShapeDtypeStruct((R, D), BF),
            jax.ShapeDtypeStruct((R, D), BF),
            jax.ShapeDtypeStruct((RM - R, 2 * D), BF),
        ),
        in_specs=[VM],
        out_specs=(VM, VM, VM),
        name="unpack_cross",
    )(x)


def unpack_qkv_kernel(x_ref, out_ref):
    G, R, W3 = x_ref.shape
    W = W3 // 3
    for j in range(G):
        for t in range(3):
            out_ref[:, (t * G + j) * W : (t * G + j + 1) * W] = x_ref[j, :, t * W : (t + 1) * W]


def unpack_qkv(x):
    G, R, W3 = x.shape
    return pl.pallas_call(
        unpack_qkv_kernel,
        out_shape=jax.ShapeDtypeStruct((R, G * W3), BF),
        in_specs=[VM],
        out_specs=VM,
        name="unpack_qkv",
    )(x)


def exchange(x):
    return lax.all_to_all(x, GROUP, split_axis=0, concat_axis=0, tiled=True)


def body(self_qkv, cross_query, thermal_kv, owners, grad_out):
    seq_size, head_size = lax.axis_size("seq"), lax.axis_size("head")
    G = seq_size * head_size
    R = self_qkv.shape[1]
    half = thermal_kv.shape[2] // 2
    side = lax.axis_index("seq") % 2
    owner = owners[0]
    owner_seq, owner_head = owner // head_size, owner % head_size
    thermal = thermal_kv[0, 0]
    handed = lax.dynamic_slice_in_dim(thermal, (1 - side) * half, half, axis=0)
    got = lax.ppermute(handed, "seq", [(s, s ^ 1) for s in range(seq_size)])
    pick = jnp.stack([side, (owner_seq % 2 == side).astype(jnp.int32)])
    pair = owner_seq - owner_seq % 2
    sources = jnp.stack([pair * head_size + owner_head, (pair + 1) * head_size + owner_head])
    qkv = exchange(pack_qkv(self_qkv[0], G))
    rest = exchange(pack_rest(pick, cross_query[0], grad_out[0], thermal, got, G))
    pT, oT = self_fwd(qkv)
    out, ag = cross(sources, oT, rest, R)
    out_back = exchange(out)
    dqkv_back = exchange(self_bwd(qkv, pT, oT, ag))
    combined, grad_cross, grad_thermal = unpack_cross(out_back, R)
    grad_qkv = unpack_qkv(dqkv_back)
    return (combined[None], grad_qkv[None], grad_cross[None], grad_thermal[None])


def solution(mesh):
    rows = P("img", GROUP, None)
    return jax.shard_map(
        body,
        mesh=mesh,
        in_specs=(rows, rows, P("img", GROUP, None, None), P("img"), rows),
        out_specs=(rows, rows, rows, rows),
        check_vma=False,
    )
```

```python
import functools
import math

import jax
import jax.numpy as jnp
from jax import lax
from jax.experimental import pallas as pl
from jax.experimental.pallas import tpu as pltpu
from jax.sharding import PartitionSpec as P

BF = jnp.bfloat16
F32 = jnp.float32
HD = 64
GROUP = ("seq", "head")
VM = pl.BlockSpec(memory_space=pltpu.VMEM)
SM = pl.BlockSpec(memory_space=pltpu.SMEM)
SCALE = 1.0 / math.sqrt(HD)
MIB = 1 << 20


def sds(shape, dtype=BF):
    return jax.ShapeDtypeStruct(shape, dtype)


def call(kernel, name, ins, outs, mib, scratch=(), cost=None):
    smem = [a.dtype == jnp.int32 for a in ins]
    return pl.pallas_call(
        kernel,
        out_shape=outs,
        in_specs=[SM if s else VM for s in smem],
        out_specs=jax.tree.map(lambda _: VM, outs),
        scratch_shapes=scratch,
        name=name,
        cost_estimate=cost,
        compiler_params=pltpu.CompilerParams(vmem_limit_bytes=mib * MIB),
    )(*ins)


def dot(a, b):
    return jnp.dot(a, b, preferred_element_type=F32)


def dot_nt(a, b):
    return lax.dot_general(a, b, (((1,), (1,)), ((), ())), preferred_element_type=F32)


def head_only(x, h):
    if x.shape[-1] == HD:
        return x
    lane = lax.broadcasted_iota(jnp.int32, x.shape, 1)
    return jnp.where((lane >= h * HD) & (lane < (h + 1) * HD), x, jnp.zeros_like(x))


def softmax_t(scores):
    top = jnp.max(scores, axis=0, keepdims=True)
    e = jnp.exp((scores - top) * SCALE)
    return (e * (1.0 / jnp.sum(e, axis=0, keepdims=True))).astype(BF)


def split_sides(side, pair, W):
    low, high = pair[:, :W], pair[:, W:]
    return jnp.where(side == 0, low, high), jnp.where(side == 0, high, low)


def pack_qkv_kernel(meta_ref, x_ref, *msgs):
    R, W = msgs[0].shape[0], msgs[0].shape[1] // 3
    D = x_ref.shape[1] // 3
    side = meta_ref[0]
    for d in range(len(msgs) - 1):
        for t in range(3):
            start = pl.multiple_of(t * D + meta_ref[1 + d] * 2 * W, 2 * W)
            mine, other = split_sides(side, x_ref[:, pl.ds(start, 2 * W)], W)
            lanes = slice(t * W, (t + 1) * W)
            if d == 0:
                msgs[0][:, lanes] = mine
                msgs[1][:, lanes] = other
            else:
                msgs[d + 1][0, :, lanes] = mine
                msgs[d + 1][1, :, lanes] = other


def pack_rest_kernel(meta_ref, cq_ref, go_ref, t_ref, got_ref, *msgs):
    R, D = cq_ref.shape
    half = got_ref.shape[0]
    W = msgs[0].shape[1] // 2
    C = len(msgs) - 1
    side = meta_ref[0]
    own_rows = pl.ds(pl.multiple_of(side * half, half), half)
    keep = meta_ref[2 + C] == 1
    for d in range(C):
        for t in range(4):
            at = meta_ref[1 + d] * 2 * W
            if t == 0:
                pair = cq_ref[:, pl.ds(pl.multiple_of(at, 2 * W), 2 * W)]
            elif t == 1:
                pair = go_ref[:, pl.ds(pl.multiple_of(at, 2 * W), 2 * W)]
            else:
                cols = pl.ds(pl.multiple_of((t - 2) * D + at, 2 * W), 2 * W)
                pair = jnp.where(keep, t_ref[own_rows, cols], got_ref[:, cols])
            mine, other = split_sides(side, pair, W)
            rows = slice(0, R) if t < 2 else slice(R, R + half)
            lanes = slice((t % 2) * W, (t % 2 + 1) * W)
            if d == 0:
                msgs[0][rows, lanes] = mine
                msgs[1][rows, lanes] = other
            else:
                msgs[d + 1][0, rows, lanes] = mine
                msgs[d + 1][1, rows, lanes] = other


def message_shapes(C, rows, width, dtype=BF):
    return (sds((rows, width), dtype),) * 2 + (sds((2, rows, width), dtype),) * (C - 1)


def pieces(refs):
    C = len(refs) // 2
    out = []
    for d in range(C):
        if d == 0:
            out.append(lambda *ix, ref=refs[0]: ref[ix])
        else:
            out.append(lambda *ix, ref=refs[d]: ref[(0,) + ix])
        out.append(lambda *ix, ref=refs[C + d]: ref[ix])
    return out


def put(msgs, block, rows, lanes, value):
    d, e = block // 2, block % 2
    if d == 0:
        msgs[e][rows, lanes] = value
    else:
        msgs[d + 1][e, rows, lanes] = value


def self_fwd_kernel(*refs, C):
    blocks = pieces(refs[: 2 * C])
    pT_ref, oT_ref, k_ref, vT_ref = refs[2 * C :]
    L, W = k_ref.shape
    R = L // len(blocks)
    QB = 2 * R
    every = slice(None)
    for i, block in enumerate(blocks):
        k_ref[i * R : (i + 1) * R] = block(every, slice(W, 2 * W))
        vT_ref[:, i * R : (i + 1) * R] = block(every, slice(2 * W, 3 * W)).T
    k = k_ref[...]
    for b in range(C):
        q = jnp.concatenate([block(every, slice(0, W)) for block in blocks[2 * b : 2 * b + 2]])
        cols = slice(b * QB, (b + 1) * QB)
        for h in range(W // HD):
            rows = slice(h * HD, (h + 1) * HD)
            p = softmax_t(dot_nt(k, head_only(q, h)))
            pT_ref[h, :, cols] = p
            oT_ref[rows, cols] = dot(vT_ref[rows, :], p)


def cross_kernel(meta_ref, oT_ref, *refs, C):
    blocks = pieces(refs[: 2 * C])
    msgs = refs[2 * C : 3 * C + 1]
    ag_ref, t_ref, dt_ref = refs[3 * C + 1 :]
    W, L = oT_ref.shape
    M = t_ref.shape[0]
    half = M // 2
    R = L // len(blocks)
    QB = 2 * R
    every = slice(None)
    side = meta_ref[0]
    here = meta_ref[1 + C]
    for d in range(C):

        @pl.when(here == d)
        def _():
            t_ref[pl.ds(pl.multiple_of(side * half, half), half), :] = blocks[2 * d](slice(R, None), every)
            t_ref[pl.ds(pl.multiple_of((1 - side) * half, half), half), :] = blocks[2 * d + 1](
                slice(R, None), every
            )

    tk, tv = t_ref[:, :W], t_ref[:, W:]
    tkT, tvT = tk.T, tv.T
    dtk = dtv = None
    for b in range(C):
        pair = blocks[2 * b : 2 * b + 2]
        cq = jnp.concatenate([block(slice(0, R), slice(0, W)) for block in pair])
        go = jnp.concatenate([block(slice(0, R), slice(W, 2 * W)) for block in pair])
        att = oT_ref[:, b * QB : (b + 1) * QB].T.astype(BF).astype(F32)
        goT = go.T.astype(F32)
        x = (att + cq.astype(F32)).astype(BF)
        mixed, dqs = [], []
        for h in range(W // HD):
            rows = slice(h * HD, (h + 1) * HD)
            xh, gh = head_only(x, h), head_only(go, h)
            p = softmax_t(dot_nt(tk, xh))
            mix = dot(tvT[rows], p)
            delta = jnp.sum(goT[rows] * mix, axis=0, keepdims=True)
            ds = (p.astype(F32) * (dot_nt(tv, gh) - delta)).astype(BF)
            mixed.append(mix)
            dqs.append(dot(tkT[rows], ds))
            a, v = dot(ds, xh), dot(p, gh)
            dtk = a if dtk is None else dtk + a
            dtv = v if dtv is None else dtv + v
        dq = jnp.concatenate(dqs, axis=0).T * SCALE
        combined = (att + jnp.concatenate(mixed, axis=0).T).astype(BF)
        grad_cross = dq.astype(BF)
        ag_ref[b * QB : (b + 1) * QB] = (go.astype(F32) + dq).astype(BF)
        for e in range(2):
            part = slice(e * R, (e + 1) * R)
            put(msgs, 2 * b + e, slice(0, R), slice(0, W), combined[part])
            put(msgs, 2 * b + e, slice(0, R), slice(W, 2 * W), grad_cross[part])
    dt_ref[:, :W] = (dtk * SCALE).astype(BF)
    dt_ref[:, W:] = dtv.astype(BF)
    MR = M // (2 * C)
    for i in range(2 * C):
        start = pl.multiple_of(meta_ref[3 + C + i] * MR, MR)
        put(msgs, i, slice(R, R + MR), every, dt_ref[pl.ds(start, MR), :])


def self_bwd_kernel(*refs, C):
    blocks = pieces(refs[: 2 * C])
    pT_ref, oT_ref, ag_ref = refs[2 * C : 2 * C + 3]
    msgs = refs[2 * C + 3 : 3 * C + 4]
    v_ref, kT_ref, dk_ref, dv_ref = refs[3 * C + 4 :]
    L, W = v_ref.shape
    R = L // len(blocks)
    QB = 2 * R
    every = slice(None)
    for i, block in enumerate(blocks):
        v_ref[i * R : (i + 1) * R] = block(every, slice(2 * W, 3 * W))
        kT_ref[:, i * R : (i + 1) * R] = block(every, slice(W, 2 * W)).T
    v = v_ref[...]
    for b in range(C):
        cols = slice(b * QB, (b + 1) * QB)
        ag = ag_ref[cols]
        q = jnp.concatenate([block(every, slice(0, W)) for block in blocks[2 * b : 2 * b + 2]])
        product = ag.T.astype(F32) * oT_ref[:, cols]
        dqs = []
        for h in range(W // HD):
            rows = slice(h * HD, (h + 1) * HD)
            delta = jnp.sum(product[rows], axis=0, keepdims=True)
            agh = head_only(ag, h)
            p = pT_ref[h, :, cols]
            dv = dot(p, agh)
            ds = (p.astype(F32) * (dot_nt(v, agh) - delta)).astype(BF)
            dk = dot(ds, head_only(q, h))
            dqs.append(dot(kT_ref[rows, :], ds))
            if b == 0 and h == 0:
                dk_ref[...] = dk
                dv_ref[...] = dv
            else:
                dk_ref[...] += dk
                dv_ref[...] += dv
        dq = (jnp.concatenate(dqs, axis=0).T * SCALE).astype(BF)
        for e in range(2):
            put(msgs, 2 * b + e, every, slice(0, W), dq[e * R : (e + 1) * R])
    for i in range(len(blocks)):
        part = slice(i * R, (i + 1) * R)
        put(msgs, i, every, slice(W, 2 * W), (dk_ref[part] * SCALE).astype(BF))
        put(msgs, i, every, slice(2 * W, 3 * W), dv_ref[part].astype(BF))


def unpack_qkv_kernel(meta_ref, *refs, C):
    blocks = pieces(refs[: 2 * C])
    out_ref = refs[2 * C]
    D = out_ref.shape[1] // 3
    W = D // (2 * C)
    side = meta_ref[0]
    for d in range(C):
        for t in range(3):
            lanes = slice(t * W, (t + 1) * W)
            a, b = blocks[2 * d](slice(None), lanes), blocks[2 * d + 1](slice(None), lanes)
            start = pl.multiple_of(t * D + meta_ref[1 + d] * 2 * W, 2 * W)
            pair = jnp.concatenate([jnp.where(side == 0, a, b), jnp.where(side == 0, b, a)], axis=1)
            out_ref[:, pl.ds(start, 2 * W)] = pair


def unpack_cross_kernel(meta_ref, *refs, C):
    blocks = pieces(refs[: 2 * C])
    comb_ref, dcq_ref, dt_ref = refs[2 * C :]
    R, D = comb_ref.shape
    W = D // (2 * C)
    side = meta_ref[0]
    for d in range(C):
        for t in range(4):
            lanes = slice((t % 2) * W, (t % 2 + 1) * W)
            rows = slice(0, R) if t < 2 else slice(R, None)
            a, b = blocks[2 * d](rows, lanes), blocks[2 * d + 1](rows, lanes)
            pair = jnp.concatenate([jnp.where(side == 0, a, b), jnp.where(side == 0, b, a)], axis=1)
            at = meta_ref[1 + d] * 2 * W + (D if t == 3 else 0)
            cols = pl.ds(pl.multiple_of(at, 2 * W), 2 * W)
            (comb_ref, dcq_ref, dt_ref, dt_ref)[t][:, cols] = pair


def body(self_qkv, cross_query, thermal_kv, owners, grad_out):
    S, Hd = lax.axis_size("seq"), lax.axis_size("head")
    X = S // 2
    C = X * Hd
    R, D = cross_query.shape[1:]
    W = D // (2 * C)
    L = 2 * C * R
    M = thermal_kv.shape[2]
    half = M // 2
    MR = M // (2 * C)
    offsets = [(i, j) for j in range(Hd) for i in range(X)]
    s, h = lax.axis_index("seq"), lax.axis_index("head")
    side, x = s % 2, s // 2
    owner_s, owner_h = owners[0] // Hd, owners[0] % Hd
    away = (x - owner_s // 2 + X) % X + X * ((h - owner_h + Hd) % Hd)
    keep = (owner_s % 2 == side).astype(jnp.int32)
    chips = [((x + i) % X) * Hd + (h + j) % Hd for i, j in offsets]
    ids = []
    for i, j in offsets:
        for e in (0, 1):
            ids.append((((x - i + X) % X) * 2 + (side if e == 0 else 1 - side)) * Hd + (h - j + Hd) % Hd)
    meta = jnp.stack([side, *chips, away, keep, *ids]).astype(jnp.int32)

    def to_sibling(a):
        return lax.ppermute(a, "seq", [(i, i ^ 1) for i in range(S)])

    def to_chip(a, d, sign):
        i, j = offsets[d]
        pairs = []
        for p in range(S):
            for q in range(Hd):
                there = ((p // 2 + sign * i) % X) * 2 + p % 2
                pairs.append((p * Hd + q, there * Hd + (q + sign * j) % Hd))
        return lax.ppermute(a, GROUP, pairs)

    def exchange(msgs, sign):
        got = [to_chip(msgs[d + 1], d, sign) for d in range(1, C)]
        relayed = [to_sibling(msgs[1])] + [to_sibling(g[1]) for g in got]
        return [msgs[0], *got, *relayed]

    bind = functools.partial
    qkv = exchange(
        call(pack_qkv_kernel, "pack_qkv", [meta, self_qkv[0]], message_shapes(C, R, 3 * W), 8), 1
    )
    thermal = thermal_kv[0, 0]
    got = to_sibling(lax.dynamic_slice_in_dim(thermal, (1 - side) * half, half, axis=0))
    rest = exchange(
        call(
            pack_rest_kernel,
            "pack_rest",
            [meta, cross_query[0], grad_out[0], thermal, got],
            message_shapes(C, R + half, 2 * W),
            8,
        ),
        1,
    )
    pT, oT = call(
        bind(self_fwd_kernel, C=C),
        "self_fwd",
        qkv,
        (sds((W // HD, L, L)), sds((W, L), F32)),
        24,
        [pltpu.VMEM((L, W), BF), pltpu.VMEM((W, L), BF)],
    )
    *out, ag = call(
        bind(cross_kernel, C=C),
        "cross",
        [meta, oT, *rest],
        (*message_shapes(C, R + MR, 2 * W), sds((L, W))),
        12,
        [pltpu.VMEM((M, 2 * W), BF), pltpu.VMEM((M, 2 * W), BF)],
    )
    out = exchange(out, -1)
    dqkv = call(
        bind(self_bwd_kernel, C=C),
        "self_bwd",
        [*qkv, pT, oT, ag],
        message_shapes(C, R, 3 * W),
        24,
        [
            pltpu.VMEM((L, W), BF),
            pltpu.VMEM((W, L), BF),
            pltpu.VMEM((L, W), F32),
            pltpu.VMEM((L, W), F32),
        ],
    )
    dqkv = exchange(dqkv, -1)
    combined, grad_cross, grad_thermal = call(
        bind(unpack_cross_kernel, C=C),
        "unpack_cross",
        [meta, *out],
        (sds((R, D)), sds((R, D)), sds((MR, 2 * D))),
        8,
    )
    grad_qkv = call(
        bind(unpack_qkv_kernel, C=C), "unpack_qkv", [meta, *dqkv], sds((R, 3 * D)), 8
    )
    return (combined[None], grad_qkv[None], grad_cross[None], grad_thermal[None])


def solution(mesh):
    rows = P("img", GROUP, None)
    return jax.shard_map(
        body,
        mesh=mesh,
        in_specs=(rows, rows, P("img", GROUP, None, None), P("img"), rows),
        out_specs=(rows, rows, rows, rows),
        check_vma=False,
    )
```

```python
import functools
import math

import jax
import jax.numpy as jnp
from jax import lax
from jax.experimental import pallas as pl
from jax.experimental.pallas import tpu as pltpu
from jax.sharding import PartitionSpec as P

BF = jnp.bfloat16
F32 = jnp.float32
HD = 64
GROUP = ("seq", "head")
VM = pl.BlockSpec(memory_space=pltpu.VMEM)
SM = pl.BlockSpec(memory_space=pltpu.SMEM)
SCALE = 1.0 / math.sqrt(HD)
MIB = 1 << 20


def sds(shape, dtype=BF):
    return jax.ShapeDtypeStruct(shape, dtype)


def call(kernel, name, ins, outs, mib, scratch=(), cost=None):
    smem = [a.dtype == jnp.int32 for a in ins]
    return pl.pallas_call(
        kernel,
        out_shape=outs,
        in_specs=[SM if s else VM for s in smem],
        out_specs=jax.tree.map(lambda _: VM, outs),
        scratch_shapes=scratch,
        name=name,
        cost_estimate=cost,
        compiler_params=pltpu.CompilerParams(vmem_limit_bytes=mib * MIB),
    )(*ins)


def cost(scores, products):
    return pl.CostEstimate(
        flops=2 * 256 * scores * products, bytes_accessed=4 * scores, transcendentals=scores
    )


def dot(a, b):
    return jnp.dot(a, b, preferred_element_type=F32)


def dot_nt(a, b):
    return lax.dot_general(a, b, (((1,), (1,)), ((), ())), preferred_element_type=F32)


def head_only(x, h):
    if x.shape[-1] == HD:
        return x
    lane = lax.broadcasted_iota(jnp.int32, x.shape, 1)
    return jnp.where((lane >= h * HD) & (lane < (h + 1) * HD), x, jnp.zeros_like(x))


def softmax_t(scores):
    top = jnp.max(scores, axis=0, keepdims=True)
    e = jnp.exp((scores - top) * SCALE)
    return (e * (1.0 / jnp.sum(e, axis=0, keepdims=True))).astype(BF)


def columns(meta_ref, d, side, base, W):
    return pl.ds(pl.multiple_of(base + meta_ref[1 + d] * 2 * W + side * W, W), W)


def pack_kernel(meta_ref, *refs, tensors, blocks, C):
    ins, msgs = refs[: 2 * blocks], refs[2 * blocks : 2 * blocks + C]
    sems = refs[-1] if len(refs) > 2 * blocks + C else None
    W = msgs[0].shape[1] // (3 if blocks == 1 else 2)
    side, keep = meta_ref[0], meta_ref[2 + C] == 1
    n = 0
    waits = []
    for d in range(C):
        for a, base, row, lane, both in tensors:
            own, sib = ins[2 * a], ins[2 * a + 1]
            rows = own.shape[0]
            lanes = slice(lane * W, (lane + 1) * W)
            if sems is None:
                at = pl.ds(pl.multiple_of(base + meta_ref[1 + d] * 2 * W, 2 * W), 2 * W)
                x, y = own[:, at], sib[:, at]
                x = jnp.where(side == 0, x[:, :W], x[:, W:])
                y = jnp.where(side == 0, y[:, :W], y[:, W:])
                if both:
                    msgs[d][row : row + rows, lanes] = x
                    msgs[d][row + rows : row + 2 * rows, lanes] = y
                else:
                    msgs[d][row : row + rows, lanes] = jnp.where(keep, x, y)
                continue
            at = columns(meta_ref, d, side, base, W)
            first = pltpu.make_async_copy(
                own.at[:, at], msgs[d].at[pl.ds(row, rows), lanes], sems.at[n]
            )
            second = pltpu.make_async_copy(
                sib.at[:, at],
                msgs[d].at[pl.ds(row + rows if both else row, rows), lanes],
                sems.at[n + 1 if both else n],
            )
            if both:
                first.start()
                second.start()
                waits += [first, second]
                n += 2
            else:
                pl.when(keep)(first.start)
                pl.when(jnp.logical_not(keep))(second.start)
                waits.append(first)
                n += 1
    for copy in waits:
        copy.wait()


def pack(name, meta, pairs, tensors, C, rows, width):
    W = width // (3 if len(pairs) == 1 else 2)
    direct = W % 128 == 0
    n = C * sum(2 if t[4] else 1 for t in tensors)
    space = pl.BlockSpec(memory_space=pl.ANY) if direct else VM
    return pl.pallas_call(
        functools.partial(pack_kernel, tensors=tensors, blocks=len(pairs), C=C),
        out_shape=(sds((rows, width)),) * C,
        in_specs=[SM] + [space] * (2 * len(pairs)),
        out_specs=(VM,) * C,
        scratch_shapes=[pltpu.SemaphoreType.DMA((n,))] if direct else [],
        name=name,
        compiler_params=pltpu.CompilerParams(vmem_limit_bytes=8 * MIB),
    )(meta, *[a for pair in pairs for a in pair])


def message_shapes(C, rows, width, dtype=BF):
    return (sds((rows, width), dtype),) * 2 + (sds((2, rows, width), dtype),) * (C - 1)


def pieces(refs):
    C = len(refs) // 2
    out = []
    for d in range(C):
        if d == 0:
            out.append(lambda *ix, ref=refs[0]: ref[ix])
        else:
            out.append(lambda *ix, ref=refs[d]: ref[(0,) + ix])
        out.append(lambda *ix, ref=refs[C + d]: ref[ix])
    return out


def put(msgs, block, rows, lanes, value):
    d, e = block // 2, block % 2
    if d == 0:
        msgs[e][rows, lanes] = value
    else:
        msgs[d + 1][e, rows, lanes] = value


def self_fwd_kernel(*refs, C):
    qkv = refs[:C]
    pT_ref, oT_ref, k_ref, vT_ref = refs[C:]
    L, W = k_ref.shape
    QB = L // C
    for b in range(C):
        k_ref[b * QB : (b + 1) * QB] = qkv[b][:, W : 2 * W]
        vT_ref[:, b * QB : (b + 1) * QB] = qkv[b][:, 2 * W :].T
    k = k_ref[...]
    for b in range(C):
        q = qkv[b][:, :W]
        cols = slice(b * QB, (b + 1) * QB)
        for h in range(W // HD):
            rows = slice(h * HD, (h + 1) * HD)
            p = softmax_t(dot_nt(k, head_only(q, h)))
            pT_ref[h, :, cols] = p
            oT_ref[rows, cols] = dot(vT_ref[rows, :], p)


def cross_kernel(meta_ref, oT_ref, *refs, C):
    rest = refs[:C]
    msgs = refs[C : 2 * C + 1]
    ag_ref, t_ref, dt_ref = refs[2 * C + 1 :]
    W, L = oT_ref.shape
    M = t_ref.shape[0]
    QB = L // C
    R = QB // 2
    every = slice(None)
    here = meta_ref[1 + C]
    for d in range(C):

        @pl.when(here == d)
        def _():
            t_ref[...] = rest[d][QB:, :]

    tk, tv = t_ref[:, :W], t_ref[:, W:]
    tkT, tvT = tk.T, tv.T
    dtk = dtv = None
    for b in range(C):
        cq, go = rest[b][:QB, :W], rest[b][:QB, W:]
        att = oT_ref[:, b * QB : (b + 1) * QB].T.astype(BF).astype(F32)
        goT = go.T.astype(F32)
        x = (att + cq.astype(F32)).astype(BF)
        mixed, dqs = [], []
        for h in range(W // HD):
            rows = slice(h * HD, (h + 1) * HD)
            xh, gh = head_only(x, h), head_only(go, h)
            p = softmax_t(dot_nt(tk, xh))
            mix = dot(tvT[rows], p)
            delta = jnp.sum(goT[rows] * mix, axis=0, keepdims=True)
            ds = (p.astype(F32) * (dot_nt(tv, gh) - delta)).astype(BF)
            mixed.append(mix)
            dqs.append(dot(tkT[rows], ds))
            a, v = dot(ds, xh), dot(p, gh)
            dtk = a if dtk is None else dtk + a
            dtv = v if dtv is None else dtv + v
        dq = jnp.concatenate(dqs, axis=0).T * SCALE
        combined = (att + jnp.concatenate(mixed, axis=0).T).astype(BF)
        grad_cross = dq.astype(BF)
        ag_ref[b * QB : (b + 1) * QB] = (go.astype(F32) + dq).astype(BF)
        for e in range(2):
            part = slice(e * R, (e + 1) * R)
            put(msgs, 2 * b + e, slice(0, R), slice(0, W), combined[part])
            put(msgs, 2 * b + e, slice(0, R), slice(W, 2 * W), grad_cross[part])
    dt_ref[:, :W] = (dtk * SCALE).astype(BF)
    dt_ref[:, W:] = dtv.astype(BF)
    MR = M // (2 * C)
    for i in range(2 * C):
        start = pl.multiple_of(meta_ref[3 + C + i] * MR, MR)
        put(msgs, i, slice(R, R + MR), every, dt_ref[pl.ds(start, MR), :])


def self_bwd_kernel(*refs, C):
    qkv = refs[:C]
    pT_ref, oT_ref, ag_ref = refs[C : C + 3]
    msgs = refs[C + 3 : 2 * C + 4]
    v_ref, kT_ref, dk_ref, dv_ref = refs[2 * C + 4 :]
    L, W = v_ref.shape
    QB = L // C
    R = QB // 2
    every = slice(None)
    for b in range(C):
        v_ref[b * QB : (b + 1) * QB] = qkv[b][:, 2 * W :]
        kT_ref[:, b * QB : (b + 1) * QB] = qkv[b][:, W : 2 * W].T
    v = v_ref[...]
    for b in range(C):
        cols = slice(b * QB, (b + 1) * QB)
        ag = ag_ref[cols]
        q = qkv[b][:, :W]
        product = ag.T.astype(F32) * oT_ref[:, cols]
        dqs = []
        for h in range(W // HD):
            rows = slice(h * HD, (h + 1) * HD)
            delta = jnp.sum(product[rows], axis=0, keepdims=True)
            agh = head_only(ag, h)
            p = pT_ref[h, :, cols]
            dv = dot(p, agh)
            ds = (p.astype(F32) * (dot_nt(v, agh) - delta)).astype(BF)
            dk = dot(ds, head_only(q, h))
            dqs.append(dot(kT_ref[rows, :], ds))
            if b == 0 and h == 0:
                dk_ref[...] = dk
                dv_ref[...] = dv
            else:
                dk_ref[...] += dk
                dv_ref[...] += dv
        dq = (jnp.concatenate(dqs, axis=0).T * SCALE).astype(BF)
        for e in range(2):
            put(msgs, 2 * b + e, every, slice(0, W), dq[e * R : (e + 1) * R])
    for i in range(2 * C):
        part = slice(i * R, (i + 1) * R)
        put(msgs, i, every, slice(W, 2 * W), (dk_ref[part] * SCALE).astype(BF))
        put(msgs, i, every, slice(2 * W, 3 * W), dv_ref[part].astype(BF))


def unpack_kernel(meta_ref, *refs, tensors, outs, C):
    blocks = pieces(refs[: 2 * C])
    targets = refs[2 * C : 2 * C + outs]
    sems = refs[-1] if len(refs) > 2 * C + outs else None
    W = refs[0].shape[1] // (3 if outs == 1 else 2)
    side = meta_ref[0]
    copies = []
    for d in range(C):
        for o, base, rows, lane in tensors:
            lanes = slice(lane * W, (lane + 1) * W)
            if sems is None:
                a, b = blocks[2 * d](rows, lanes), blocks[2 * d + 1](rows, lanes)
                start = pl.multiple_of(base + meta_ref[1 + d] * 2 * W, 2 * W)
                pair = [jnp.where(side == 0, a, b), jnp.where(side == 0, b, a)]
                targets[o][:, pl.ds(start, 2 * W)] = jnp.concatenate(pair, axis=1)
                continue
            direct = refs[0] if d == 0 else refs[d].at[0]
            for source, at in ((direct, side), (refs[C + d], 1 - side)):
                copies.append(
                    pltpu.make_async_copy(
                        source.at[rows, lanes],
                        targets[o].at[:, columns(meta_ref, d, at, base, W)],
                        sems.at[len(copies)],
                    )
                )
                copies[-1].start()
    for copy in copies:
        copy.wait()


def unpack(name, meta, arrays, tensors, outs, C):
    W = arrays[0].shape[1] // (3 if len(outs) == 1 else 2)
    direct = W % 128 == 0
    space = pl.BlockSpec(memory_space=pl.ANY) if direct else VM
    sems = [pltpu.SemaphoreType.DMA((2 * C * len(tensors),))] if direct else []
    return pl.pallas_call(
        functools.partial(unpack_kernel, tensors=tensors, outs=len(outs), C=C),
        out_shape=outs,
        in_specs=[SM] + [VM] * (2 * C),
        out_specs=(space,) * len(outs),
        scratch_shapes=sems,
        name=name,
        compiler_params=pltpu.CompilerParams(vmem_limit_bytes=8 * MIB),
    )(meta, *arrays)


def body(self_qkv, cross_query, thermal_kv, owners, grad_out):
    S, Hd = lax.axis_size("seq"), lax.axis_size("head")
    X = S // 2
    C = X * Hd
    R, D = cross_query.shape[1:]
    W = D // (2 * C)
    L = 2 * C * R
    M = thermal_kv.shape[2]
    MR = M // (2 * C)
    offsets = [(i, j) for j in range(Hd) for i in range(X)]
    s, h = lax.axis_index("seq"), lax.axis_index("head")
    side, x = s % 2, s // 2
    owner_s, owner_h = owners[0] // Hd, owners[0] % Hd
    away = (x - owner_s // 2 + X) % X + X * ((h - owner_h + Hd) % Hd)
    keep = (owner_s % 2 == side).astype(jnp.int32)
    chips = [((x + i) % X) * Hd + (h + j) % Hd for i, j in offsets]
    ids = []
    for i, j in offsets:
        for e in (0, 1):
            ids.append((((x - i + X) % X) * 2 + (side if e == 0 else 1 - side)) * Hd + (h - j + Hd) % Hd)
    meta = jnp.stack([side, *chips, away, keep, *ids]).astype(jnp.int32)

    def to_sibling(a):
        return lax.ppermute(a, "seq", [(i, i ^ 1) for i in range(S)])

    def to_chip(a, d, sign):
        i, j = offsets[d]
        pairs = []
        for p in range(S):
            for q in range(Hd):
                there = ((p // 2 + sign * i) % X) * 2 + p % 2
                pairs.append((p * Hd + q, there * Hd + (q + sign * j) % Hd))
        return lax.ppermute(a, GROUP, pairs)

    def send(msgs, sign):
        return [to_chip(msgs[d + 1], d, sign) for d in range(1, C)], to_sibling(msgs[1])

    def relay(msgs, got, sibling):
        return [msgs[0], *got, sibling, *[to_sibling(g[1]) for g in got]]

    def after(arrays, *gates):
        return lax.optimization_barrier((list(arrays), gates))[0]

    bind = functools.partial
    heads = W // HD
    x_pair = (self_qkv[0], to_sibling(self_qkv[0]))
    cq_pair = (cross_query[0], to_sibling(cross_query[0]))
    go_pair = (grad_out[0], to_sibling(grad_out[0]))
    t_pair = (thermal_kv[0, 0], to_sibling(thermal_kv[0, 0]))
    msgs = pack(
        "pack_qkv", meta, [x_pair], [(0, t * D, 0, t, True) for t in range(3)], C, 2 * R, 3 * W
    )
    got = [to_chip(msgs[d], d, 1) for d in range(1, C)]
    rest = pack(
        "pack_rest",
        meta,
        [cq_pair, go_pair, t_pair],
        [
            (0, 0, 0, 0, True),
            (1, 0, 0, 1, True),
            (2, 0, 2 * R, 0, False),
            (2, D, 2 * R, 1, False),
        ],
        C,
        2 * R + M,
        2 * W,
    )
    got = after(got, *rest)
    rest = after(rest, got[0])
    rest_got = [to_chip(rest[d], d, 1) for d in range(1, C)]
    qkv = [msgs[0], *got]
    pT, oT = call(
        bind(self_fwd_kernel, C=C),
        "self_fwd",
        qkv,
        (sds((heads, L, L)), sds((W, L), F32)),
        24,
        [pltpu.VMEM((L, W), BF), pltpu.VMEM((W, L), BF)],
        cost(heads * L * L, 2),
    )
    rest = [rest[0], *after(rest_got, oT)]
    *out, ag = call(
        bind(cross_kernel, C=C),
        "cross",
        [meta, oT, *rest],
        (*message_shapes(C, R + MR, 2 * W), sds((L, W))),
        12,
        [pltpu.VMEM((M, 2 * W), BF), pltpu.VMEM((M, 2 * W), BF)],
        cost(heads * L * M, 6),
    )
    out_got, out_sibling = send(out, -1)
    dqkv = call(
        bind(self_bwd_kernel, C=C),
        "self_bwd",
        [*qkv, pT, oT, ag],
        message_shapes(C, R, 3 * W),
        24,
        [
            pltpu.VMEM((L, W), BF),
            pltpu.VMEM((W, L), BF),
            pltpu.VMEM((L, W), F32),
            pltpu.VMEM((L, W), F32),
        ],
        cost(heads * L * L, 4),
    )
    dqkv_got, dqkv_sibling = send(dqkv, -1)
    out = relay(out, after(out_got, dqkv[0]), out_sibling)
    combined, grad_cross, grad_thermal = unpack(
        "unpack_cross",
        meta,
        out,
        [
            (0, 0, slice(0, R), 0),
            (1, 0, slice(0, R), 1),
            (2, 0, slice(R, R + MR), 0),
            (2, D, slice(R, R + MR), 1),
        ],
        (sds((R, D)), sds((R, D)), sds((MR, 2 * D))),
        C,
    )
    (first_relay,) = [to_sibling(g[1]) for g in dqkv_got[:1]]
    later = after(dqkv_got[1:], combined, first_relay)
    dqkv = [dqkv[0], dqkv_got[0], *later, dqkv_sibling, first_relay, *[to_sibling(g[1]) for g in later]]
    (grad_qkv,) = unpack(
        "unpack_qkv",
        meta,
        dqkv,
        [(0, t * D, slice(None), t) for t in range(3)],
        (sds((R, 3 * D)),),
        C,
    )
    return (combined[None], grad_qkv[None], grad_cross[None], grad_thermal[None])


def solution(mesh):
    rows = P("img", GROUP, None)
    return jax.shard_map(
        body,
        mesh=mesh,
        in_specs=(rows, rows, P("img", GROUP, None, None), P("img"), rows),
        out_specs=(rows, rows, rows, rows),
        check_vma=False,
    )
```

```python
import functools
import math

import jax
import jax.numpy as jnp
from jax import lax
from jax.experimental import pallas as pl
from jax.experimental.pallas import tpu as pltpu
from jax.sharding import PartitionSpec as P

BF = jnp.bfloat16
F32 = jnp.float32
HD = 64
GROUP = ("seq", "head")
VM = pl.BlockSpec(memory_space=pltpu.VMEM)
SM = pl.BlockSpec(memory_space=pltpu.SMEM)
SCALE = 1.0 / math.sqrt(HD)
MIB = 1 << 20


def sds(shape, dtype=BF):
    return jax.ShapeDtypeStruct(shape, dtype)


def call(kernel, name, ins, outs, mib, scratch=(), cost=None):
    smem = [a.dtype == jnp.int32 for a in ins]
    return pl.pallas_call(
        kernel,
        out_shape=outs,
        in_specs=[SM if s else VM for s in smem],
        out_specs=jax.tree.map(lambda _: VM, outs),
        scratch_shapes=scratch,
        name=name,
        cost_estimate=cost,
        compiler_params=pltpu.CompilerParams(vmem_limit_bytes=mib * MIB),
    )(*ins)


def cost(scores, products):
    return pl.CostEstimate(
        flops=2 * 256 * scores * products, bytes_accessed=4 * scores, transcendentals=scores
    )


def dot(a, b):
    return jnp.dot(a, b, preferred_element_type=F32)


def dot_nt(a, b):
    return lax.dot_general(a, b, (((1,), (1,)), ((), ())), preferred_element_type=F32)


def softmax_t(scores):
    top = jnp.max(scores, axis=0, keepdims=True)
    e = jnp.exp((scores - top) * SCALE)
    return (e * (1.0 / jnp.sum(e, axis=0, keepdims=True))).astype(BF)


def head_columns(meta_ref, d, ref, base, p, W):
    at = base + meta_ref[1 + d] * 2 * W
    if W == HD:
        block = ref[:, pl.ds(pl.multiple_of(at, 128), 128)]
        return jnp.where(meta_ref[0] == 0, block[:, :HD], block[:, HD:])
    at = at + meta_ref[0] * W + (p // 2) * 128
    half = slice((p % 2) * HD, (p % 2 + 1) * HD)
    return ref[:, pl.ds(pl.multiple_of(at, 128), 128)][:, half]


def beside(a, b):
    return jnp.concatenate([a, b], axis=1)


def pack_own_kernel(meta_ref, x_ref, cq_ref, out_ref, *, p):
    C, R2, _ = out_ref.shape
    R, D = cq_ref.shape
    W = D // (2 * C)
    for d in range(C):
        cols = functools.partial(head_columns, meta_ref, d, p=p, W=W)
        out_ref[d, :R] = beside(cols(x_ref, 0), cols(x_ref, D))
        out_ref[d, R:] = beside(cols(x_ref, 2 * D), cols(cq_ref, 0))


def pack_sib_kernel(meta_ref, own_ref, go_ref, t_ref, xs_ref, cqs_ref, gos_ref, ts_ref, *msgs, p):
    C = len(msgs)
    R, D = go_ref.shape
    W = D // (2 * C)
    keep = meta_ref[2 + C] == 1
    for d in range(C):
        cols = functools.partial(head_columns, meta_ref, d, p=p, W=W)
        msg = msgs[d]
        msg[:R] = own_ref[d, :R]
        msg[R : 2 * R] = beside(cols(xs_ref, 0), cols(xs_ref, D))
        msg[2 * R : 3 * R] = own_ref[d, R:]
        msg[3 * R : 4 * R] = beside(cols(xs_ref, 2 * D), cols(cqs_ref, 0))
        msg[4 * R : 5 * R] = beside(cols(go_ref, 0), cols(gos_ref, 0))
        own = beside(cols(t_ref, 0), cols(t_ref, D))
        sib = beside(cols(ts_ref, 0), cols(ts_ref, D))
        msg[5 * R :] = jnp.where(keep, own, sib)


def pieces(refs):
    C = len(refs) // 2
    out = []
    for d in range(C):
        if d == 0:
            out.append(lambda rows, lanes, ref=refs[0]: ref[rows, lanes])
        else:
            out.append(lambda rows, lanes, ref=refs[d]: ref[0, rows, lanes])
        out.append(lambda rows, lanes, ref=refs[C + d]: ref[rows, lanes])
    return out


def put(msgs, block, rows, lanes, value):
    d, e = block // 2, block % 2
    if d == 0:
        msgs[e][rows, lanes] = value
    else:
        msgs[d + 1][e, rows, lanes] = value


def message_shapes(C, rows):
    return (sds((rows, 128)),) * 2 + (sds((2, rows, 128)),) * (C - 1)


def layer_kernel(meta_ref, *refs, C, R, M):
    ins, outs = refs[:C], refs[C : 2 * C + 1]
    k_ref, v_ref, kT_ref, vT_ref, t_ref, dt_ref, dk_ref, dv_ref = refs[2 * C + 1 :]
    QB = 2 * R
    MR = M // (2 * C)
    left, right = slice(0, HD), slice(HD, 2 * HD)
    for b in range(C):
        rows = slice(b * QB, (b + 1) * QB)
        k, v = ins[b][:QB, right], ins[b][QB : 2 * QB, left]
        k_ref[rows], v_ref[rows] = k, v
        kT_ref[:, rows], vT_ref[:, rows] = k.T, v.T
    for d in range(C):

        @pl.when(meta_ref[1 + C] == d)
        def _():
            t_ref[...] = ins[d][5 * R :, :]

    tk, tv = t_ref[:, left], t_ref[:, right]
    tkT, tvT = tk.T, tv.T
    k, v, kT, vT = k_ref[...], v_ref[...], kT_ref[...], vT_ref[...]
    dtk = dtv = None
    for b in range(C):
        q, cq = ins[b][:QB, left], ins[b][QB : 2 * QB, right]
        go = ins[b][4 * R : 5 * R, :]
        go = jnp.concatenate([go[:, left], go[:, right]], axis=0)
        p = softmax_t(dot_nt(k, q))
        oT = dot(vT, p)
        att = oT.T.astype(BF).astype(F32)
        x = (att + cq.astype(F32)).astype(BF)
        cp = softmax_t(dot_nt(tk, x))
        mix = dot(tvT, cp)
        delta = jnp.sum(go.T.astype(F32) * mix, axis=0, keepdims=True)
        ds = (cp.astype(F32) * (dot_nt(tv, go) - delta)).astype(BF)
        dq = dot(tkT, ds).T * SCALE
        a, c = dot(ds, x), dot(cp, go)
        dtk = a if dtk is None else dtk + a
        dtv = c if dtv is None else dtv + c
        combined, dcq = (att + mix.T).astype(BF), dq.astype(BF)
        ag = (go.astype(F32) + dq).astype(BF)
        delta = jnp.sum(ag.T.astype(F32) * oT, axis=0, keepdims=True)
        ds = (p.astype(F32) * (dot_nt(v, ag) - delta)).astype(BF)
        dk, dv = dot(ds, q), dot(p, ag)
        if b == 0:
            dk_ref[...] = dk
            dv_ref[...] = dv
        else:
            dk_ref[...] += dk
            dv_ref[...] += dv
        dq = (dot(kT, ds).T * SCALE).astype(BF)
        for e in range(2):
            part = slice(e * R, (e + 1) * R)
            put(outs, 2 * b + e, slice(0, R), left, dq[part])
            put(outs, 2 * b + e, slice(R, 2 * R), right, combined[part])
            h = R // 2
            put(
                outs,
                2 * b + e,
                slice(2 * R, 2 * R + h),
                slice(None),
                beside(dcq[e * R : e * R + h], dcq[e * R + h : (e + 1) * R]),
            )
    dt_ref[...] = beside(dtk * SCALE, dtv).astype(BF)
    for i in range(2 * C):
        part = slice(i * R, (i + 1) * R)
        put(outs, i, slice(0, R), right, (dk_ref[part] * SCALE).astype(BF))
        put(outs, i, slice(R, 2 * R), left, dv_ref[part].astype(BF))
        start = pl.multiple_of(meta_ref[3 + C + i] * MR, MR)
        put(outs, i, slice(2 * R + R // 2, None), slice(None), dt_ref[pl.ds(start, MR), :])


def unpack_kernel(meta_ref, *refs, C, H):
    passes = [pieces(refs[2 * C * p : 2 * C * (p + 1)]) for p in range(H)]
    qkv_ref, comb_ref, dcq_ref, dt_ref = refs[2 * C * H :]
    R, D = comb_ref.shape
    W = D // (2 * C)
    side = meta_ref[0]
    left, right = slice(0, HD), slice(HD, 2 * HD)
    first, second = slice(0, R), slice(R, 2 * R)
    low, high, end = (
        slice(2 * R, 2 * R + R // 2),
        slice(2 * R, 2 * R + R // 2),
        slice(2 * R + R // 2, None),
    )

    def dcq(piece):
        return jnp.concatenate([piece(low, left), piece(high, right)], axis=0)

    parts = [
        (qkv_ref, 0, lambda piece: piece(first, left)),
        (qkv_ref, D, lambda piece: piece(first, right)),
        (qkv_ref, 2 * D, lambda piece: piece(second, left)),
        (comb_ref, 0, lambda piece: piece(second, right)),
        (dcq_ref, 0, dcq),
        (dt_ref, 0, lambda piece: piece(end, left)),
        (dt_ref, D, lambda piece: piece(end, right)),
    ]
    for d in range(C):
        for ref, base, read in parts:
            at = base + meta_ref[1 + d] * 2 * W
            if H == 1:
                a, b = read(passes[0][2 * d]), read(passes[0][2 * d + 1])
                pair = beside(jnp.where(side == 0, a, b), jnp.where(side == 0, b, a))
                ref[:, pl.ds(pl.multiple_of(at, 128), 128)] = pair
                continue
            for e in range(2):
                core = side if e == 0 else 1 - side
                for p in range(0, H, 2):
                    pair = beside(read(passes[p][2 * d + e]), read(passes[p + 1][2 * d + e]))
                    start = pl.multiple_of(at + core * W + p * HD, 128)
                    ref[:, pl.ds(start, 128)] = pair


def body(self_qkv, cross_query, thermal_kv, owners, grad_out):
    S, Hd = lax.axis_size("seq"), lax.axis_size("head")
    X = S // 2
    C = X * Hd
    R, D = cross_query.shape[1:]
    W = D // (2 * C)
    L = 2 * C * R
    M = thermal_kv.shape[2]
    MR = M // (2 * C)
    offsets = [(i, j) for j in range(Hd) for i in range(X)]
    s, h = lax.axis_index("seq"), lax.axis_index("head")
    side, x = s % 2, s // 2
    owner_s, owner_h = owners[0] // Hd, owners[0] % Hd
    away = (x - owner_s // 2 + X) % X + X * ((h - owner_h + Hd) % Hd)
    keep = (owner_s % 2 == side).astype(jnp.int32)
    chips = [((x + i) % X) * Hd + (h + j) % Hd for i, j in offsets]
    ids = []
    for i, j in offsets:
        for e in (0, 1):
            ids.append((((x - i + X) % X) * 2 + (side if e == 0 else 1 - side)) * Hd + (h - j + Hd) % Hd)
    meta = jnp.stack([side, *chips, away, keep, *ids]).astype(jnp.int32)

    def to_sibling(a):
        return lax.ppermute(a, "seq", [(i, i ^ 1) for i in range(S)])

    def to_chip(a, d, sign):
        i, j = offsets[d]
        pairs = []
        for p in range(S):
            for q in range(Hd):
                there = ((p // 2 + sign * i) % X) * 2 + p % 2
                pairs.append((p * Hd + q, there * Hd + (q + sign * j) % Hd))
        return lax.ppermute(a, GROUP, pairs)

    def after(arrays, *gates):
        return lax.optimization_barrier((list(arrays), gates))[0]

    bind = functools.partial
    H = W // HD
    RO = 2 * R + R // 2 + MR
    own = (self_qkv[0], cross_query[0], grad_out[0], thermal_kv[0, 0])
    xs, cqs, gos, ts = [to_sibling(a) for a in own]
    x, cq, go, t = own
    msgs, got = [], []
    for p in range(H):
        if p:
            x, cq = after([x, cq], *msgs[p - 1])
        half = call(
            bind(pack_own_kernel, p=p), f"pack_own_{p}", [meta, x, cq], sds((C, 2 * R, 128)), 8
        )
        msgs.append(
            call(
                bind(pack_sib_kernel, p=p),
                f"pack_sib_{p}",
                [meta, half, go, t, xs, cqs, gos, ts],
                (sds((5 * R + M, 128)),) * C,
                12,
            )
        )
        got.append([to_chip(msgs[p][d], d, 1) for d in range(1, C)])
        if p:
            got[p - 1] = after(got[p - 1], *msgs[p])
    backs, outs = [], []
    for p in range(H):
        out = call(
            bind(layer_kernel, C=C, R=R, M=M),
            f"layer_{p}",
            [meta, msgs[p][0], *got[p]],
            message_shapes(C, RO),
            32,
            [pltpu.VMEM((L, HD), BF)] * 2
            + [pltpu.VMEM((HD, L), BF)] * 2
            + [pltpu.VMEM((M, 128), BF)] * 2
            + [pltpu.VMEM((L, HD), F32)] * 2,
            cost(L * L + L * M, 6),
        )
        outs.append(out)
        if p + 1 < H:
            got[p + 1] = after(got[p + 1], *out)
        backs.append([to_chip(out[d + 1], d, -1) for d in range(1, C)])
    pieces_in = []
    for p in range(H):
        back = after(backs[p], outs[p + 1][0]) if p + 1 < H else backs[p]
        relayed = [to_sibling(outs[p][1])] + [to_sibling(g[1]) for g in back]
        if p + 1 < H:
            backs[p + 1] = after(backs[p + 1], *relayed)
        pieces_in += [outs[p][0], *back, *relayed]
    grad_qkv, combined, grad_cross, grad_thermal = call(
        bind(unpack_kernel, C=C, H=H),
        "unpack",
        [meta, *pieces_in],
        (sds((R, 3 * D)), sds((R, D)), sds((R, D)), sds((MR, 2 * D))),
        12,
    )
    return (combined[None], grad_qkv[None], grad_cross[None], grad_thermal[None])


def solution(mesh):
    rows = P("img", GROUP, None)
    return jax.shard_map(
        body,
        mesh=mesh,
        in_specs=(rows, rows, P("img", GROUP, None, None), P("img"), rows),
        out_specs=(rows, rows, rows, rows),
        check_vma=False,
    )
```

```python
import functools
import math

import jax
import jax.numpy as jnp
from jax import lax
from jax.experimental import pallas as pl
from jax.experimental.pallas import tpu as pltpu
from jax.sharding import PartitionSpec as P

BF = jnp.bfloat16
F32 = jnp.float32
HD = 64
GROUP = ("seq", "head")
VM = pl.BlockSpec(memory_space=pltpu.VMEM)
SM = pl.BlockSpec(memory_space=pltpu.SMEM)
SCALE = 1.0 / math.sqrt(HD)
MIB = 1 << 20
LIMIT = 36


def sds(shape, dtype=BF):
    return jax.ShapeDtypeStruct(shape, dtype)


def call(kernel, name, ins, outs, mib, scratch=(), cost=None):
    smem = [a.dtype == jnp.int32 for a in ins]
    return pl.pallas_call(
        kernel,
        out_shape=outs,
        in_specs=[SM if s else VM for s in smem],
        out_specs=jax.tree.map(lambda _: VM, outs),
        scratch_shapes=scratch,
        name=name,
        cost_estimate=cost,
        compiler_params=pltpu.CompilerParams(vmem_limit_bytes=mib * MIB),
    )(*ins)


def cost(scores, products):
    return pl.CostEstimate(
        flops=2 * 256 * scores * products, bytes_accessed=4 * scores, transcendentals=scores
    )


def dot(a, b):
    return jnp.dot(a, b, preferred_element_type=F32)


def dot_nt(a, b):
    return lax.dot_general(a, b, (((1,), (1,)), ((), ())), preferred_element_type=F32)


def softmax_t(scores):
    top = jnp.max(scores, axis=0, keepdims=True)
    e = jnp.exp2((scores - top) * (SCALE * math.log2(math.e)))
    return (e * (1.0 / jnp.sum(e, axis=0, keepdims=True))).astype(BF)


def head_columns(meta_ref, d, ref, base, p, W):
    at = base + meta_ref[1 + d] * 2 * W
    if W == HD:
        block = ref[:, pl.ds(pl.multiple_of(at, 128), 128)]
        return jnp.where(meta_ref[0] == 0, block[:, :HD], block[:, HD:])
    at = at + meta_ref[0] * W + (p // 2) * 128
    half = slice((p % 2) * HD, (p % 2 + 1) * HD)
    return ref[:, pl.ds(pl.multiple_of(at, 128), 128)][:, half]


def beside(a, b):
    return jnp.concatenate([a, b], axis=1)


def pack_own_kernel(meta_ref, x_ref, cq_ref, out_ref, *, p):
    C, R2, _ = out_ref.shape
    R, D = cq_ref.shape
    W = D // (2 * C)
    for d in range(C):
        cols = functools.partial(head_columns, meta_ref, d, p=p, W=W)
        out_ref[d, :R] = beside(cols(x_ref, 0), cols(x_ref, D))
        out_ref[d, R:] = beside(cols(x_ref, 2 * D), cols(cq_ref, 0))


def pack_sib_kernel(meta_ref, own_ref, go_ref, t_ref, xs_ref, cqs_ref, gos_ref, ts_ref, *msgs, p):
    C = len(msgs)
    R, D = go_ref.shape
    W = D // (2 * C)
    keep = meta_ref[2 + C] == 1
    for d in range(C):
        cols = functools.partial(head_columns, meta_ref, d, p=p, W=W)
        msg = msgs[d]
        msg[:R] = own_ref[d, :R]
        msg[R : 2 * R] = beside(cols(xs_ref, 0), cols(xs_ref, D))
        msg[2 * R : 3 * R] = own_ref[d, R:]
        msg[3 * R : 4 * R] = beside(cols(xs_ref, 2 * D), cols(cqs_ref, 0))
        msg[4 * R : 5 * R] = beside(cols(go_ref, 0), cols(gos_ref, 0))
        own = beside(cols(t_ref, 0), cols(t_ref, D))
        sib = beside(cols(ts_ref, 0), cols(ts_ref, D))
        msg[5 * R :] = jnp.where(keep, own, sib)


def pieces(refs):
    C = len(refs) // 2
    out = []
    for d in range(C):
        if d == 0:
            out.append(lambda rows, lanes, ref=refs[0]: ref[rows, lanes])
        else:
            out.append(lambda rows, lanes, ref=refs[d]: ref[0, rows, lanes])
        out.append(lambda rows, lanes, ref=refs[C + d]: ref[rows, lanes])
    return out


def put(msgs, block, rows, lanes, value):
    d, e = block // 2, block % 2
    if d == 0:
        msgs[e][rows, lanes] = value
    else:
        msgs[d + 1][e, rows, lanes] = value


def message_shapes(C, rows):
    return (sds((rows, 128)),) * 2 + (sds((2, rows, 128)),) * (C - 1)


def ahead(count, first, rest):
    value = first(0)
    for i in range(count):
        following = first(i + 1) if i + 1 < count else None
        rest(i, value)
        value = following


def layer_kernel(meta_ref, *refs, C, R, M):
    ins, outs = refs[:C], refs[C : 2 * C + 1]
    q_ref, k_ref, v_ref, cq_ref, go_ref, vT_ref, kT_ref, t_ref, dt_ref = refs[2 * C + 1 : 2 * C + 10]
    oT_ref, ag_ref, pT_ref, ds_ref = refs[2 * C + 10 :]
    L = 2 * C * R
    QB = 2 * R
    MR = M // (2 * C)
    left, right = slice(0, HD), slice(HD, 2 * HD)
    for b in range(C):
        rows = slice(b * QB, (b + 1) * QB)
        q_ref[rows], k_ref[rows] = ins[b][:QB, left], ins[b][:QB, right]
        v_ref[rows], cq_ref[rows] = ins[b][QB : 2 * QB, left], ins[b][QB : 2 * QB, right]
        go_ref[b * QB : b * QB + R] = ins[b][4 * R : 5 * R, left]
        go_ref[b * QB + R : (b + 1) * QB] = ins[b][4 * R : 5 * R, right]
        kT_ref[:, rows], vT_ref[:, rows] = k_ref[rows].T, v_ref[rows].T
    for d in range(C):

        @pl.when(meta_ref[1 + C] == d)
        def _():
            t_ref[...] = ins[d][5 * R :, :]

    tk, tv = t_ref[:, left], t_ref[:, right]
    tkT, tvT = tk.T, tv.T
    k, v, kT, vT = k_ref[...], v_ref[...], kT_ref[...], vT_ref[...]

    WB = 512

    def block(b):
        return slice(b * WB, (b + 1) * WB)

    def attend(b, scores):
        p = softmax_t(scores)
        pT_ref[:, block(b)] = p
        oT_ref[:, block(b)] = dot(vT, p)

    ahead(L // WB, lambda b: dot_nt(k, q_ref[block(b)]), attend)
    go = go_ref[...]
    att = oT_ref[...].T.astype(BF).astype(F32)
    x = (att + cq_ref[...].astype(F32)).astype(BF)
    cp = softmax_t(dot_nt(tk, x))
    dp = dot_nt(tv, go)
    mix = dot(tvT, cp)
    delta = jnp.sum(go.T.astype(F32) * mix, axis=0, keepdims=True)
    ds = (cp.astype(F32) * (dp - delta)).astype(BF)
    dq = dot(tkT, ds).T * SCALE
    ag = (go.astype(F32) + dq).astype(BF)
    ag_ref[...] = ag
    dt_ref[...] = beside(dot(ds, x) * SCALE, dot(cp, go)).astype(BF)
    combined, dcq = (att + mix.T).astype(BF), dq.astype(BF)
    h = R // 2
    for i in range(2 * C):
        at = i * R
        put(outs, i, slice(R, 2 * R), right, combined[at : at + R])
        halves = beside(dcq[at : at + h], dcq[at + h : at + R])
        put(outs, i, slice(2 * R, 2 * R + h), slice(None), halves)
        start = pl.multiple_of(meta_ref[3 + C + i] * MR, MR)
        put(outs, i, slice(2 * R + h, None), slice(None), dt_ref[pl.ds(start, MR), :])
    delta = jnp.sum(ag.T.astype(F32) * oT_ref[...], axis=0, keepdims=True)

    def back(b, dp):
        ds = (pT_ref[:, block(b)].astype(F32) * (dp - delta[:, block(b)])).astype(BF)
        ds_ref[:, block(b)] = ds
        dq = (dot(kT, ds).T * SCALE).astype(BF)
        n = WB // R
        for e in range(n):
            put(outs, n * b + e, slice(0, R), left, dq[e * R : (e + 1) * R])

    ahead(L // WB, lambda b: dot_nt(v, ag_ref[block(b)]), back)
    dk = (dot(ds_ref[...], q_ref[...]) * SCALE).astype(BF)
    dv = dot(pT_ref[...], ag).astype(BF)
    for i in range(2 * C):
        part = slice(i * R, (i + 1) * R)
        put(outs, i, slice(0, R), right, dk[part])
        put(outs, i, slice(R, 2 * R), left, dv[part])


def layer(meta, msgs, C, R, M):
    L, H = 2 * C * R, HD
    return call(
        functools.partial(layer_kernel, C=C, R=R, M=M),
        "layer",
        [meta, *msgs],
        message_shapes(C, 2 * R + R // 2 + M // (2 * C)),
        LIMIT,
        [pltpu.VMEM((L, H), BF)] * 5
        + [pltpu.VMEM((H, L), BF)] * 2
        + [pltpu.VMEM((M, 128), BF)] * 2
        + [pltpu.VMEM((H, L), F32), pltpu.VMEM((L, H), BF)]
        + [pltpu.VMEM((L, L), BF)] * 2,
        cost(L * L + L * M, 6),
    )


def unpack_kernel(meta_ref, *refs, C, H):
    passes = [pieces(refs[2 * C * p : 2 * C * (p + 1)]) for p in range(H)]
    qkv_ref, comb_ref, dcq_ref, dt_ref = refs[2 * C * H :]
    R, D = comb_ref.shape
    W = D // (2 * C)
    side = meta_ref[0]
    left, right = slice(0, HD), slice(HD, 2 * HD)
    first, second = slice(0, R), slice(R, 2 * R)
    low, high, end = (
        slice(2 * R, 2 * R + R // 2),
        slice(2 * R, 2 * R + R // 2),
        slice(2 * R + R // 2, None),
    )

    def dcq(piece):
        return jnp.concatenate([piece(low, left), piece(high, right)], axis=0)

    parts = [
        (qkv_ref, 0, lambda piece: piece(first, left)),
        (qkv_ref, D, lambda piece: piece(first, right)),
        (qkv_ref, 2 * D, lambda piece: piece(second, left)),
        (comb_ref, 0, lambda piece: piece(second, right)),
        (dcq_ref, 0, dcq),
        (dt_ref, 0, lambda piece: piece(end, left)),
        (dt_ref, D, lambda piece: piece(end, right)),
    ]
    for d in range(C):
        for ref, base, read in parts:
            at = base + meta_ref[1 + d] * 2 * W
            if H == 1:
                a, b = read(passes[0][2 * d]), read(passes[0][2 * d + 1])
                pair = beside(jnp.where(side == 0, a, b), jnp.where(side == 0, b, a))
                ref[:, pl.ds(pl.multiple_of(at, 128), 128)] = pair
                continue
            for e in range(2):
                core = side if e == 0 else 1 - side
                for p in range(0, H, 2):
                    pair = beside(read(passes[p][2 * d + e]), read(passes[p + 1][2 * d + e]))
                    start = pl.multiple_of(at + core * W + p * HD, 128)
                    ref[:, pl.ds(start, 128)] = pair


def body(self_qkv, cross_query, thermal_kv, owners, grad_out):
    S, Hd = lax.axis_size("seq"), lax.axis_size("head")
    X = S // 2
    C = X * Hd
    R, D = cross_query.shape[1:]
    W = D // (2 * C)
    M = thermal_kv.shape[2]
    MR = M // (2 * C)
    offsets = [(i, j) for j in range(Hd) for i in range(X)]
    s, h = lax.axis_index("seq"), lax.axis_index("head")
    side, x = s % 2, s // 2
    owner_s, owner_h = owners[0] // Hd, owners[0] % Hd
    away = (x - owner_s // 2 + X) % X + X * ((h - owner_h + Hd) % Hd)
    keep = (owner_s % 2 == side).astype(jnp.int32)
    chips = [((x + i) % X) * Hd + (h + j) % Hd for i, j in offsets]
    ids = []
    for i, j in offsets:
        for e in (0, 1):
            ids.append((((x - i + X) % X) * 2 + (side if e == 0 else 1 - side)) * Hd + (h - j + Hd) % Hd)
    meta = jnp.stack([side, *chips, away, keep, *ids]).astype(jnp.int32)

    def to_sibling(a):
        return lax.ppermute(a, "seq", [(i, i ^ 1) for i in range(S)])

    def to_chip(a, d, sign):
        i, j = offsets[d]
        pairs = []
        for p in range(S):
            for q in range(Hd):
                there = ((p // 2 + sign * i) % X) * 2 + p % 2
                pairs.append((p * Hd + q, there * Hd + (q + sign * j) % Hd))
        return lax.ppermute(a, GROUP, pairs)

    def after(arrays, *gates):
        return lax.optimization_barrier((list(arrays), gates))[0]

    bind = functools.partial
    H = W // HD
    own = (self_qkv[0], cross_query[0], grad_out[0], thermal_kv[0, 0])
    xs, cqs, gos, ts = [to_sibling(a) for a in own]
    x, cq, go, t = own
    msgs, got = [], []
    for p in range(H):
        if p:
            x, cq = after([x, cq], *msgs[p - 1])
        half = call(
            bind(pack_own_kernel, p=p), f"pack_own_{p}", [meta, x, cq], sds((C, 2 * R, 128)), 8
        )
        msgs.append(
            call(
                bind(pack_sib_kernel, p=p),
                f"pack_sib_{p}",
                [meta, half, go, t, xs, cqs, gos, ts],
                (sds((5 * R + M, 128)),) * C,
                12,
            )
        )
        got.append([to_chip(msgs[p][d], d, 1) for d in range(1, C)])
        if p:
            got[p - 1] = after(got[p - 1], *msgs[p])
    backs, outs = [], []
    for p in range(H):
        out = layer(meta, [msgs[p][0], *got[p]], C, R, M)
        outs.append(out)
        if p + 1 < H:
            got[p + 1] = after(got[p + 1], *out)
        backs.append([to_chip(out[d + 1], d, -1) for d in range(1, C)])
    pieces_in = []
    for p in range(H):
        back = after(backs[p], outs[p + 1][0]) if p + 1 < H else backs[p]
        relayed = [to_sibling(outs[p][1])] + [to_sibling(g[1]) for g in back]
        if p + 1 < H:
            backs[p + 1] = after(backs[p + 1], *relayed)
        pieces_in += [outs[p][0], *back, *relayed]
    grad_qkv, combined, grad_cross, grad_thermal = call(
        bind(unpack_kernel, C=C, H=H),
        "unpack",
        [meta, *pieces_in],
        (sds((R, 3 * D)), sds((R, D)), sds((R, D)), sds((MR, 2 * D))),
        12,
    )
    return (combined[None], grad_qkv[None], grad_cross[None], grad_thermal[None])


def solution(mesh):
    rows = P("img", GROUP, None)
    return jax.shard_map(
        body,
        mesh=mesh,
        in_specs=(rows, rows, P("img", GROUP, None, None), P("img"), rows),
        out_specs=(rows, rows, rows, rows),
        check_vma=False,
    )
```

```python
import functools
import math

import jax
import jax.numpy as jnp
from jax import lax
from jax.experimental import pallas as pl
from jax.experimental.pallas import tpu as pltpu
from jax.sharding import PartitionSpec as P

BF = jnp.bfloat16
F32 = jnp.float32
HD = 64
GROUP = ("seq", "head")
VM = pl.BlockSpec(memory_space=pltpu.VMEM)
SM = pl.BlockSpec(memory_space=pltpu.SMEM)
SCALE = 1.0 / math.sqrt(HD)
MIB = 1 << 20
LIMIT = 36


def sds(shape, dtype=BF):
    return jax.ShapeDtypeStruct(shape, dtype)


def call(kernel, name, ins, outs, mib, scratch=(), cost=None):
    smem = [a.dtype == jnp.int32 for a in ins]
    return pl.pallas_call(
        kernel,
        out_shape=outs,
        in_specs=[SM if s else VM for s in smem],
        out_specs=jax.tree.map(lambda _: VM, outs),
        scratch_shapes=scratch,
        name=name,
        cost_estimate=cost,
        compiler_params=pltpu.CompilerParams(vmem_limit_bytes=mib * MIB),
    )(*ins)


def cost(scores, products):
    return pl.CostEstimate(
        flops=2 * 256 * scores * products, bytes_accessed=4 * scores, transcendentals=scores
    )


def dot(a, b):
    return jnp.dot(a, b, preferred_element_type=F32)


def dot_nt(a, b):
    return lax.dot_general(a, b, (((1,), (1,)), ((), ())), preferred_element_type=F32)


def softmax_t(scores):
    top = jnp.max(scores, axis=0, keepdims=True)
    e = jnp.exp2((scores - top) * (SCALE * math.log2(math.e)))
    return (e * (1.0 / jnp.sum(e, axis=0, keepdims=True))).astype(BF)


def head_columns(meta_ref, d, ref, base, p, W):
    at = base + meta_ref[1 + d] * 2 * W
    if W == HD:
        block = ref[:, pl.ds(pl.multiple_of(at, 128), 128)]
        return jnp.where(meta_ref[0] == 0, block[:, :HD], block[:, HD:])
    at = at + meta_ref[0] * W + (p // 2) * 128
    half = slice((p % 2) * HD, (p % 2 + 1) * HD)
    return ref[:, pl.ds(pl.multiple_of(at, 128), 128)][:, half]


def beside(a, b):
    return jnp.concatenate([a, b], axis=1)


def pack_own_kernel(meta_ref, x_ref, cq_ref, out_ref, *, p):
    C, R2, _ = out_ref.shape
    R, D = cq_ref.shape
    W = D // (2 * C)
    for d in range(C):
        cols = functools.partial(head_columns, meta_ref, d, p=p, W=W)
        out_ref[d, :R] = beside(cols(x_ref, D), cols(x_ref, 0))
        out_ref[d, R:] = beside(cols(x_ref, 2 * D), cols(cq_ref, 0))


def pack_sib_kernel(meta_ref, own_ref, go_ref, t_ref, xs_ref, cqs_ref, gos_ref, ts_ref, *msgs, p):
    C = len(msgs)
    R, D = go_ref.shape
    W = D // (2 * C)
    keep = meta_ref[2 + C] == 1
    for d in range(C):
        cols = functools.partial(head_columns, meta_ref, d, p=p, W=W)
        msg = msgs[d]
        msg[:R] = own_ref[d, :R]
        msg[R : 2 * R] = beside(cols(xs_ref, D), cols(xs_ref, 0))
        msg[2 * R : 3 * R] = own_ref[d, R:]
        msg[3 * R : 4 * R] = beside(cols(xs_ref, 2 * D), cols(cqs_ref, 0))
        msg[4 * R : 5 * R] = beside(cols(go_ref, 0), cols(gos_ref, 0))
        own = beside(cols(t_ref, 0), cols(t_ref, D))
        sib = beside(cols(ts_ref, 0), cols(ts_ref, D))
        msg[5 * R :] = jnp.where(keep, own, sib)


def pieces(refs):
    C = len(refs) // 2
    out = []
    for d in range(C):
        if d == 0:
            out.append(lambda rows, lanes, ref=refs[0]: ref[rows, lanes])
        else:
            lead = (0,) if len(refs[d].shape) == 3 else ()
            out.append(lambda rows, lanes, ref=refs[d], lead=lead: ref[(*lead, rows, lanes)])
        out.append(lambda rows, lanes, ref=refs[C + d]: ref[rows, lanes])
    return out


def put(msgs, block, rows, lanes, value):
    d, e = block // 2, block % 2
    if d == 0 or len(msgs[-1].shape) == 2:
        msgs[block][rows, lanes] = value
    else:
        msgs[d + 1][e, rows, lanes] = value


def message_shapes(C, rows, direct):
    if direct:
        return (sds((rows, 128)),) * (2 * C)
    return (sds((rows, 128)),) * 2 + (sds((2, rows, 128)),) * (C - 1)


def ahead(count, first, rest):
    value = first(0)
    for i in range(count):
        following = first(i + 1) if i + 1 < count else None
        rest(i, value)
        value = following


def layer_kernel(meta_ref, *refs, C, R, M):
    ins, outs = refs[:C], refs[C:-14]
    k_ref, v_ref, qT_ref, kT_ref, vT_ref, cqT_ref, goT_ref, agT_ref = refs[-14:-6]
    t_ref, dt_ref, oT_ref, back_ref, pT_ref, ds_ref = refs[-6:]
    L = 2 * C * R
    QB = 2 * R
    WB = min(512, L)
    MR = M // (2 * C)
    left, right = slice(0, HD), slice(HD, 2 * HD)
    for b in range(C):
        rows = slice(b * QB, (b + 1) * QB)
        k_ref[rows], v_ref[rows] = ins[b][:QB, left], ins[b][QB : 2 * QB, left]
        both = ins[b][:QB].T
        kT_ref[:, rows], qT_ref[:, rows] = both[left], both[right]
        both = ins[b][QB : 2 * QB].T
        vT_ref[:, rows], cqT_ref[:, rows] = both[left], both[right]
        both = ins[b][4 * R : 5 * R].T
        goT_ref[:, b * QB : b * QB + R], goT_ref[:, b * QB + R : (b + 1) * QB] = both[left], both[right]
    for d in range(C):

        @pl.when(meta_ref[1 + C] == d)
        def _():
            t_ref[...] = ins[d][5 * R :, :]

    tk, tv = t_ref[:, left], t_ref[:, right]
    tT = t_ref[...].T
    tkT, tvT = tT[left], tT[right]
    k, v, kT, vT = k_ref[...], v_ref[...], kT_ref[...], vT_ref[...]

    def block(b):
        return slice(b * WB, (b + 1) * WB)

    def attend(b, scores):
        p = softmax_t(scores)
        pT_ref[:, block(b)] = p
        oT_ref[:, block(b)] = dot(vT, p)

    ahead(L // WB, lambda b: dot(k, qT_ref[:, block(b)]), attend)
    goT = goT_ref[...]
    wide = goT.astype(F32)
    att = oT_ref[...].astype(BF).astype(F32)
    xT = (att + cqT_ref[...].astype(F32)).astype(BF)
    dp = dot(tv, goT)
    cp = softmax_t(dot(tk, xT))
    mix = dot(tvT, cp)
    back_ref[right] = (att + mix).astype(BF)
    delta = jnp.sum(wide * mix, axis=0, keepdims=True)
    ds = (cp.astype(F32) * (dp - delta)).astype(BF)
    dq = dot(tkT, ds) * SCALE
    agT = (wide + dq).astype(BF)
    agT_ref[...] = agT
    dcq = dq.astype(BF)
    dt_ref[...] = beside(dot_nt(ds, xT) * SCALE, dot_nt(cp, goT)).astype(BF)
    h = R // 2
    for i in range(2 * C):
        at = i * R
        halves = jnp.concatenate([dcq[:, at : at + h], dcq[:, at + h : at + R]], axis=0)
        put(outs, i, slice(2 * R, 2 * R + h), slice(None), halves.T)
        start = pl.multiple_of(meta_ref[3 + C + i] * MR, MR)
        put(outs, i, slice(2 * R + h, None), slice(None), dt_ref[pl.ds(start, MR), :])
    delta = jnp.sum(agT.astype(F32) * oT_ref[...], axis=0, keepdims=True)

    def back(b, dp):
        ds = (pT_ref[:, block(b)].astype(F32) * (dp - delta[:, block(b)])).astype(BF)
        ds_ref[:, block(b)] = ds
        back_ref[left, block(b)] = (dot(kT, ds) * SCALE).astype(BF)
        n = WB // R
        for i in range(n * b, n * b + n):
            put(outs, i, slice(0, R), slice(None), back_ref[:, i * R : (i + 1) * R].T)

    ahead(L // WB, lambda b: dot(v, agT_ref[:, block(b)]), back)
    dk = dot(ds_ref[...], qT_ref[...].T) * SCALE
    dv = dot(pT_ref[...], agT.T)
    both = beside(dk.astype(BF), dv.astype(BF))
    for i in range(2 * C):
        put(outs, i, slice(R, 2 * R), slice(None), both[i * R : (i + 1) * R])


def layer(meta, msgs, C, R, M, direct):
    L, H = 2 * C * R, HD
    return call(
        functools.partial(layer_kernel, C=C, R=R, M=M),
        "layer",
        [meta, *msgs],
        message_shapes(C, 2 * R + R // 2 + M // (2 * C), direct),
        LIMIT,
        [pltpu.VMEM((L, H), BF)] * 2
        + [pltpu.VMEM((H, L), BF)] * 6
        + [pltpu.VMEM((M, 128), BF)] * 2
        + [pltpu.VMEM((H, L), F32), pltpu.VMEM((128, L), BF)]
        + [pltpu.VMEM((L, L), BF)] * 2,
        cost(L * L + L * M, 6),
    )


def unpack_kernel(meta_ref, *refs, C, H):
    passes = [pieces(refs[2 * C * p : 2 * C * (p + 1)]) for p in range(H)]
    outs, (qkv_ref, comb_ref, dcq_ref, dt_ref) = refs[2 * C * H :][:4], refs[2 * C * H :][4:8]
    sems = refs[-1]
    R, D = comb_ref.shape
    W = D // (2 * C)
    side = meta_ref[0]
    left, right = slice(0, HD), slice(HD, 2 * HD)
    first, second = slice(0, R), slice(R, 2 * R)
    low, high, end = (
        slice(2 * R, 2 * R + R // 2),
        slice(2 * R, 2 * R + R // 2),
        slice(2 * R + R // 2, None),
    )

    def dcq(piece):
        return jnp.concatenate([piece(low, left), piece(high, right)], axis=0)

    parts = [
        (qkv_ref, 0, lambda piece: piece(first, left)),
        (qkv_ref, D, lambda piece: piece(second, left)),
        (qkv_ref, 2 * D, lambda piece: piece(second, right)),
        (comb_ref, 0, lambda piece: piece(first, right)),
        (dcq_ref, 0, dcq),
        (dt_ref, 0, lambda piece: piece(end, left)),
        (dt_ref, D, lambda piece: piece(end, right)),
    ]
    copies = []
    for n, (ref, base, read) in enumerate(parts):
        for d in range(C):
            at = base + meta_ref[1 + d] * 2 * W
            if H == 1:
                a, b = read(passes[0][2 * d]), read(passes[0][2 * d + 1])
                pair = beside(jnp.where(side == 0, a, b), jnp.where(side == 0, b, a))
                ref[:, pl.ds(pl.multiple_of(at, 128), 128)] = pair
                continue
            for e in range(2):
                core = side if e == 0 else 1 - side
                for p in range(0, H, 2):
                    pair = beside(read(passes[p][2 * d + e]), read(passes[p + 1][2 * d + e]))
                    start = pl.multiple_of(at + core * W + p * HD, 128)
                    ref[:, pl.ds(start, 128)] = pair
        target = outs[(0, 0, 0, 1, 2, 3, 3)[n]]
        cols = slice(base, base + D)
        copies.append(pltpu.make_async_copy(ref.at[:, cols], target.at[:, cols], sems.at[n]))
        copies[-1].start()
    for copy in copies:
        copy.wait()


def body(self_qkv, cross_query, thermal_kv, owners, grad_out):
    S, Hd = lax.axis_size("seq"), lax.axis_size("head")
    X = S // 2
    C = X * Hd
    R, D = cross_query.shape[1:]
    W = D // (2 * C)
    M = thermal_kv.shape[2]
    MR = M // (2 * C)
    offsets = [(i, j) for j in range(Hd) for i in range(X)]
    s, h = lax.axis_index("seq"), lax.axis_index("head")
    side, x = s % 2, s // 2
    owner_s, owner_h = owners[0] // Hd, owners[0] % Hd
    away = (x - owner_s // 2 + X) % X + X * ((h - owner_h + Hd) % Hd)
    keep = (owner_s % 2 == side).astype(jnp.int32)
    chips = [((x + i) % X) * Hd + (h + j) % Hd for i, j in offsets]
    ids = []
    for i, j in offsets:
        for e in (0, 1):
            ids.append((((x - i + X) % X) * 2 + (side if e == 0 else 1 - side)) * Hd + (h - j + Hd) % Hd)
    meta = jnp.stack([side, *chips, away, keep, *ids]).astype(jnp.int32)

    def to_sibling(a):
        return lax.ppermute(a, "seq", [(i, i ^ 1) for i in range(S)])

    def to_chip(a, d, sign, other=0):
        i, j = offsets[d]
        pairs = []
        for p in range(S):
            for q in range(Hd):
                there = ((p // 2 + sign * i) % X) * 2 + (p % 2 ^ other)
                pairs.append((p * Hd + q, there * Hd + (q + sign * j) % Hd))
        return lax.ppermute(a, GROUP, pairs)

    def after(arrays, *gates):
        return lax.optimization_barrier((list(arrays), gates))[0]

    bind = functools.partial
    H = W // HD
    own = (self_qkv[0], cross_query[0], grad_out[0], thermal_kv[0, 0])
    xs, cqs, gos, ts = [to_sibling(a) for a in own]
    x, cq, go, t = own
    msgs, got = [], []
    for p in range(H):
        if p:
            x, cq = after([x, cq], *msgs[p - 1])
        half = call(
            bind(pack_own_kernel, p=p), f"pack_own_{p}", [meta, x, cq], sds((C, 2 * R, 128)), 8
        )
        msgs.append(
            call(
                bind(pack_sib_kernel, p=p),
                f"pack_sib_{p}",
                [meta, half, go, t, xs, cqs, gos, ts],
                (sds((5 * R + M, 128)),) * C,
                12,
            )
        )
        got.append([to_chip(msgs[p][d], d, 1) for d in range(1, C)])
        if p:
            got[p - 1] = after(got[p - 1], *msgs[p])
    backs, outs = [], []
    for p in range(H):
        out = layer(meta, [msgs[p][0], *got[p]], C, R, M, p == H - 1)
        outs.append(out)
        if p + 1 < H:
            got[p + 1] = after(got[p + 1], *out)
        if p + 1 < H:
            backs.append([to_chip(out[d + 1], d, -1) for d in range(1, C)])
    pieces_in = []
    for p in range(H - 1):
        back = after(backs[p], outs[p + 1][0])
        relayed = [to_sibling(outs[p][1])] + [to_sibling(g[1]) for g in back]
        pieces_in += [outs[p][0], *back, *relayed]
    out = outs[-1]
    straight = [to_chip(out[2 * d], d, -1) for d in range(1, C)]
    across = [to_chip(out[2 * d + 1], d, -1, 1) for d in range(C)]
    pieces_in += [out[0], *straight, *across]
    shapes = (sds((R, 3 * D)), sds((R, D)), sds((R, D)), sds((MR, 2 * D)))
    grad_qkv, combined, grad_cross, grad_thermal = pl.pallas_call(
        bind(unpack_kernel, C=C, H=H),
        out_shape=shapes,
        in_specs=[SM] + [VM] * len(pieces_in),
        out_specs=(pl.BlockSpec(memory_space=pltpu.HBM),) * 4,
        scratch_shapes=[pltpu.VMEM(o.shape, BF) for o in shapes] + [pltpu.SemaphoreType.DMA((7,))],
        name="unpack",
        compiler_params=pltpu.CompilerParams(vmem_limit_bytes=8 * MIB),
    )(meta, *pieces_in)
    return (combined[None], grad_qkv[None], grad_cross[None], grad_thermal[None])


def solution(mesh):
    rows = P("img", GROUP, None)
    return jax.shard_map(
        body,
        mesh=mesh,
        in_specs=(rows, rows, P("img", GROUP, None, None), P("img"), rows),
        out_specs=(rows, rows, rows, rows),
        check_vma=False,
    )
```

```python
import functools
import math

import jax
import jax.numpy as jnp
from jax import lax
from jax.experimental import pallas as pl
from jax.experimental.pallas import tpu as pltpu
from jax.sharding import PartitionSpec as P

BF = jnp.bfloat16
F32 = jnp.float32
HD = 64
GROUP = ("seq", "head")
VM = pl.BlockSpec(memory_space=pltpu.VMEM)
SM = pl.BlockSpec(memory_space=pltpu.SMEM)
SCALE = 1.0 / math.sqrt(HD)
MIB = 1 << 20
LIMIT = 36


def sds(shape, dtype=BF):
    return jax.ShapeDtypeStruct(shape, dtype)


def call(kernel, name, ins, outs, mib, scratch=(), cost=None):
    smem = [a.dtype == jnp.int32 for a in ins]
    return pl.pallas_call(
        kernel,
        out_shape=outs,
        in_specs=[SM if s else VM for s in smem],
        out_specs=jax.tree.map(lambda _: VM, outs),
        scratch_shapes=scratch,
        name=name,
        cost_estimate=cost,
        compiler_params=pltpu.CompilerParams(vmem_limit_bytes=mib * MIB),
    )(*ins)


def cost(scores, products):
    return pl.CostEstimate(
        flops=2 * 256 * scores * products, bytes_accessed=4 * scores, transcendentals=scores
    )


def dot(a, b):
    return jnp.dot(a, b, preferred_element_type=F32)


def dot_nt(a, b):
    return lax.dot_general(a, b, (((1,), (1,)), ((), ())), preferred_element_type=F32)


def softmax_t(scores):
    top = jnp.max(scores, axis=0, keepdims=True)
    e = jnp.exp2((scores - top) * (SCALE * math.log2(math.e)))
    return (e * (1.0 / jnp.sum(e, axis=0, keepdims=True))).astype(BF)


def head_columns(meta_ref, d, ref, base, p, W):
    at = base + meta_ref[1 + d] * 2 * W
    if W == HD:
        block = ref[:, pl.ds(pl.multiple_of(at, 128), 128)]
        return jnp.where(meta_ref[0] == 0, block[:, :HD], block[:, HD:])
    at = at + meta_ref[0] * W + (p // 2) * 128
    half = slice((p % 2) * HD, (p % 2 + 1) * HD)
    return ref[:, pl.ds(pl.multiple_of(at, 128), 128)][:, half]


def beside(a, b):
    return jnp.concatenate([a, b], axis=1)


def pack_own_kernel(meta_ref, x_ref, cq_ref, out_ref, *, p):
    C, R2, _ = out_ref.shape
    R, D = cq_ref.shape
    W = D // (2 * C)
    for d in range(C):
        cols = functools.partial(head_columns, meta_ref, d, p=p, W=W)
        out_ref[d, :R] = beside(cols(x_ref, D), cols(x_ref, 0))
        out_ref[d, R:] = beside(cols(x_ref, 2 * D), cols(cq_ref, 0))


def pack_sib_kernel(meta_ref, own_ref, go_ref, t_ref, xs_ref, cqs_ref, gos_ref, ts_ref, *msgs, p):
    C = len(msgs)
    R, D = go_ref.shape
    W = D // (2 * C)
    keep = meta_ref[2 + C] == 1
    for d in range(C):
        cols = functools.partial(head_columns, meta_ref, d, p=p, W=W)
        msg = msgs[d]
        msg[:R] = own_ref[d, :R]
        msg[R : 2 * R] = beside(cols(xs_ref, D), cols(xs_ref, 0))
        msg[2 * R : 3 * R] = own_ref[d, R:]
        msg[3 * R : 4 * R] = beside(cols(xs_ref, 2 * D), cols(cqs_ref, 0))
        msg[4 * R : 5 * R] = beside(cols(go_ref, 0), cols(gos_ref, 0))
        own = beside(cols(t_ref, 0), cols(t_ref, D))
        sib = beside(cols(ts_ref, 0), cols(ts_ref, D))
        msg[5 * R :] = jnp.where(keep, own, sib)


def pieces(refs):
    C = len(refs) // 2
    out = []
    for d in range(C):
        if d == 0:
            out.append(lambda rows, lanes, ref=refs[0]: ref[rows, lanes])
        else:
            lead = (0,) if len(refs[d].shape) == 3 else ()
            out.append(lambda rows, lanes, ref=refs[d], lead=lead: ref[(*lead, rows, lanes)])
        out.append(lambda rows, lanes, ref=refs[C + d]: ref[rows, lanes])
    return out


def put(msgs, block, rows, lanes, value):
    d, e = block // 2, block % 2
    if d == 0 or len(msgs[-1].shape) == 2:
        msgs[block][rows, lanes] = value
    else:
        msgs[d + 1][e, rows, lanes] = value


def message_shapes(C, rows, direct):
    if direct:
        return (sds((rows, 128)),) * (2 * C)
    return (sds((rows, 128)),) * 2 + (sds((2, rows, 128)),) * (C - 1)


def ahead(count, first, rest):
    value = first(0)
    for i in range(count):
        following = first(i + 1) if i + 1 < count else None
        rest(i, value)
        value = following


def layer_kernel(meta_ref, *refs, C, R, M):
    ins, outs = refs[:C], refs[C:-14]
    k_ref, v_ref, qT_ref, kT_ref, vT_ref, cqT_ref, goT_ref, agT_ref = refs[-14:-6]
    t_ref, dt_ref, oT_ref, back_ref, pT_ref, ds_ref = refs[-6:]
    L = 2 * C * R
    QB = 2 * R
    WB = min(512, L)
    MR = M // (2 * C)
    left, right = slice(0, HD), slice(HD, 2 * HD)
    for b in range(C):
        rows = slice(b * QB, (b + 1) * QB)
        k_ref[rows], v_ref[rows] = ins[b][:QB, left], ins[b][QB : 2 * QB, left]
        both = ins[b][:QB].T
        kT_ref[:, rows], qT_ref[:, rows] = both[left], both[right]
        both = ins[b][QB : 2 * QB].T
        vT_ref[:, rows], cqT_ref[:, rows] = both[left], both[right]
        both = ins[b][4 * R : 5 * R].T
        goT_ref[:, b * QB : b * QB + R], goT_ref[:, b * QB + R : (b + 1) * QB] = both[left], both[right]
    for d in range(C):

        @pl.when(meta_ref[1 + C] == d)
        def _():
            t_ref[...] = ins[d][5 * R :, :]

    tk, tv = t_ref[:, left], t_ref[:, right]
    tT = t_ref[...].T
    tkT, tvT = tT[left], tT[right]
    k, v, kT, vT = k_ref[...], v_ref[...], kT_ref[...], vT_ref[...]

    def block(b):
        return slice(b * WB, (b + 1) * WB)

    def attend(b, scores):
        p = softmax_t(scores)
        pT_ref[:, block(b)] = p
        oT_ref[:, block(b)] = dot(vT, p)

    ahead(L // WB, lambda b: dot(k, qT_ref[:, block(b)]), attend)
    dtk = dtv = None
    h = R // 2

    def mingle(b, products):
        nonlocal dtk, dtv
        cols = block(b)
        scores, xT, att, dp = products
        goT = goT_ref[:, cols]
        wide = goT.astype(F32)
        cp = softmax_t(scores)
        mix = dot(tvT, cp)
        back_ref[right, cols] = (att + mix).astype(BF)
        delta = jnp.sum(wide * mix, axis=0, keepdims=True)
        ds = (cp.astype(F32) * (dp - delta)).astype(BF)
        dq = dot(tkT, ds) * SCALE
        agT_ref[:, cols] = (wide + dq).astype(BF)
        dcq = dq.astype(BF)
        x, y = dot_nt(ds, xT), dot_nt(cp, goT)
        dtk, dtv = (x, y) if dtk is None else (dtk + x, dtv + y)
        for i in range(WB // R):
            at = i * R
            halves = jnp.concatenate([dcq[:, at : at + h], dcq[:, at + h : at + R]], axis=0)
            put(outs, b * (WB // R) + i, slice(2 * R, 2 * R + h), slice(None), halves.T)

    def scores_of(b):
        att = oT_ref[:, block(b)].astype(BF).astype(F32)
        xT = (att + cqT_ref[:, block(b)].astype(F32)).astype(BF)
        return dot(tk, xT), xT, att, dot(tv, goT_ref[:, block(b)])

    ahead(L // WB, scores_of, mingle)
    dt_ref[...] = beside(dtk * SCALE, dtv).astype(BF)
    for i in range(2 * C):
        start = pl.multiple_of(meta_ref[3 + C + i] * MR, MR)
        put(outs, i, slice(2 * R + h, None), slice(None), dt_ref[pl.ds(start, MR), :])
    agT = agT_ref[...]
    delta = jnp.sum(agT.astype(F32) * oT_ref[...], axis=0, keepdims=True)

    def back(b, dp):
        ds = (pT_ref[:, block(b)].astype(F32) * (dp - delta[:, block(b)])).astype(BF)
        ds_ref[:, block(b)] = ds
        back_ref[left, block(b)] = (dot(kT, ds) * SCALE).astype(BF)
        n = WB // R
        for i in range(n * b, n * b + n):
            put(outs, i, slice(0, R), slice(None), back_ref[:, i * R : (i + 1) * R].T)

    ahead(L // WB, lambda b: dot(v, agT_ref[:, block(b)]), back)
    dk = dot(ds_ref[...], qT_ref[...].T) * SCALE
    dv = dot(pT_ref[...], agT.T)
    both = beside(dk.astype(BF), dv.astype(BF))
    for i in range(2 * C):
        put(outs, i, slice(R, 2 * R), slice(None), both[i * R : (i + 1) * R])


def layer(meta, msgs, C, R, M, direct):
    L, H = 2 * C * R, HD
    return call(
        functools.partial(layer_kernel, C=C, R=R, M=M),
        "layer",
        [meta, *msgs],
        message_shapes(C, 2 * R + R // 2 + M // (2 * C), direct),
        LIMIT,
        [pltpu.VMEM((L, H), BF)] * 2
        + [pltpu.VMEM((H, L), BF)] * 6
        + [pltpu.VMEM((M, 128), BF)] * 2
        + [pltpu.VMEM((H, L), F32), pltpu.VMEM((128, L), BF)]
        + [pltpu.VMEM((L, L), BF)] * 2,
        cost(L * L + L * M, 6),
    )


def unpack_kernel(meta_ref, *refs, C, H):
    passes = [pieces(refs[2 * C * p : 2 * C * (p + 1)]) for p in range(H)]
    outs, (qkv_ref, comb_ref, dcq_ref, dt_ref) = refs[2 * C * H :][:4], refs[2 * C * H :][4:8]
    sems = refs[-1]
    R, D = comb_ref.shape
    W = D // (2 * C)
    side = meta_ref[0]
    left, right = slice(0, HD), slice(HD, 2 * HD)
    first, second = slice(0, R), slice(R, 2 * R)
    low, high, end = (
        slice(2 * R, 2 * R + R // 2),
        slice(2 * R, 2 * R + R // 2),
        slice(2 * R + R // 2, None),
    )

    def dcq(piece):
        return jnp.concatenate([piece(low, left), piece(high, right)], axis=0)

    parts = [
        (qkv_ref, 0, lambda piece: piece(first, left)),
        (qkv_ref, D, lambda piece: piece(second, left)),
        (qkv_ref, 2 * D, lambda piece: piece(second, right)),
        (comb_ref, 0, lambda piece: piece(first, right)),
        (dcq_ref, 0, dcq),
        (dt_ref, 0, lambda piece: piece(end, left)),
        (dt_ref, D, lambda piece: piece(end, right)),
    ]
    copies = []
    for n, (ref, base, read) in enumerate(parts):
        for d in range(C):
            at = base + meta_ref[1 + d] * 2 * W
            if H == 1:
                a, b = read(passes[0][2 * d]), read(passes[0][2 * d + 1])
                pair = beside(jnp.where(side == 0, a, b), jnp.where(side == 0, b, a))
                ref[:, pl.ds(pl.multiple_of(at, 128), 128)] = pair
                continue
            for e in range(2):
                core = side if e == 0 else 1 - side
                for p in range(0, H, 2):
                    pair = beside(read(passes[p][2 * d + e]), read(passes[p + 1][2 * d + e]))
                    start = pl.multiple_of(at + core * W + p * HD, 128)
                    ref[:, pl.ds(start, 128)] = pair
        target = outs[(0, 0, 0, 1, 2, 3, 3)[n]]
        cols = slice(base, base + D)
        copies.append(pltpu.make_async_copy(ref.at[:, cols], target.at[:, cols], sems.at[n]))
        copies[-1].start()
    for copy in copies:
        copy.wait()


def body(self_qkv, cross_query, thermal_kv, owners, grad_out):
    S, Hd = lax.axis_size("seq"), lax.axis_size("head")
    X = S // 2
    C = X * Hd
    R, D = cross_query.shape[1:]
    W = D // (2 * C)
    M = thermal_kv.shape[2]
    MR = M // (2 * C)
    offsets = [(i, j) for j in range(Hd) for i in range(X)]
    s, h = lax.axis_index("seq"), lax.axis_index("head")
    side, x = s % 2, s // 2
    owner_s, owner_h = owners[0] // Hd, owners[0] % Hd
    away = (x - owner_s // 2 + X) % X + X * ((h - owner_h + Hd) % Hd)
    keep = (owner_s % 2 == side).astype(jnp.int32)
    chips = [((x + i) % X) * Hd + (h + j) % Hd for i, j in offsets]
    ids = []
    for i, j in offsets:
        for e in (0, 1):
            ids.append((((x - i + X) % X) * 2 + (side if e == 0 else 1 - side)) * Hd + (h - j + Hd) % Hd)
    meta = jnp.stack([side, *chips, away, keep, *ids]).astype(jnp.int32)

    def to_sibling(a):
        return lax.ppermute(a, "seq", [(i, i ^ 1) for i in range(S)])

    def to_chip(a, d, sign, other=0):
        i, j = offsets[d]
        pairs = []
        for p in range(S):
            for q in range(Hd):
                there = ((p // 2 + sign * i) % X) * 2 + (p % 2 ^ other)
                pairs.append((p * Hd + q, there * Hd + (q + sign * j) % Hd))
        return lax.ppermute(a, GROUP, pairs)

    def after(arrays, *gates):
        return lax.optimization_barrier((list(arrays), gates))[0]

    bind = functools.partial
    H = W // HD
    own = (self_qkv[0], cross_query[0], grad_out[0], thermal_kv[0, 0])
    xs, cqs, gos, ts = [to_sibling(a) for a in own]
    x, cq, go, t = own
    msgs, got = [], []
    for p in range(H):
        if p:
            x, cq = after([x, cq], *msgs[p - 1])
        half = call(
            bind(pack_own_kernel, p=p), f"pack_own_{p}", [meta, x, cq], sds((C, 2 * R, 128)), 8
        )
        msgs.append(
            call(
                bind(pack_sib_kernel, p=p),
                f"pack_sib_{p}",
                [meta, half, go, t, xs, cqs, gos, ts],
                (sds((5 * R + M, 128)),) * C,
                12,
            )
        )
        got.append([to_chip(msgs[p][d], d, 1) for d in range(1, C)])
        if p:
            got[p - 1] = after(got[p - 1], *msgs[p])
    backs, outs = [], []
    for p in range(H):
        out = layer(meta, [msgs[p][0], *got[p]], C, R, M, p == H - 1)
        outs.append(out)
        if p + 1 < H:
            got[p + 1] = after(got[p + 1], *out)
        if p + 1 < H:
            backs.append([to_chip(out[d + 1], d, -1) for d in range(1, C)])
    pieces_in = []
    for p in range(H - 1):
        handed, *back = after([outs[p][1], *backs[p]], outs[p + 1][0])
        relayed = [to_sibling(handed)] + [to_sibling(g[1]) for g in back]
        pieces_in += [outs[p][0], *back, *relayed]
    out = outs[-1]
    straight = [to_chip(out[2 * d], d, -1) for d in range(1, C)]
    across = [to_chip(out[2 * d + 1], d, -1, 1) for d in range(C)]
    pieces_in += [out[0], *straight, *across]
    shapes = (sds((R, 3 * D)), sds((R, D)), sds((R, D)), sds((MR, 2 * D)))
    grad_qkv, combined, grad_cross, grad_thermal = pl.pallas_call(
        bind(unpack_kernel, C=C, H=H),
        out_shape=shapes,
        in_specs=[SM] + [VM] * len(pieces_in),
        out_specs=(pl.BlockSpec(memory_space=pltpu.HBM),) * 4,
        scratch_shapes=[pltpu.VMEM(o.shape, BF) for o in shapes] + [pltpu.SemaphoreType.DMA((7,))],
        name="unpack",
        compiler_params=pltpu.CompilerParams(vmem_limit_bytes=8 * MIB),
    )(meta, *pieces_in)
    return (combined[None], grad_qkv[None], grad_cross[None], grad_thermal[None])


def solution(mesh):
    rows = P("img", GROUP, None)
    return jax.shard_map(
        body,
        mesh=mesh,
        in_specs=(rows, rows, P("img", GROUP, None, None), P("img"), rows),
        out_specs=(rows, rows, rows, rows),
        check_vma=False,
    )
```

```python
import functools
import math

import jax
import jax.numpy as jnp
from jax import lax
from jax.experimental import pallas as pl
from jax.experimental.pallas import tpu as pltpu
from jax.sharding import PartitionSpec as P

BF = jnp.bfloat16
F32 = jnp.float32
HD = 64
GROUP = ("seq", "head")
VM = pl.BlockSpec(memory_space=pltpu.VMEM)
SM = pl.BlockSpec(memory_space=pltpu.SMEM)
SCALE = 1.0 / math.sqrt(HD)
MIB = 1 << 20
LIMIT = 36


def sds(shape, dtype=BF):
    return jax.ShapeDtypeStruct(shape, dtype)


def call(kernel, name, ins, outs, mib, scratch=(), cost=None):
    smem = [a.dtype == jnp.int32 for a in ins]
    return pl.pallas_call(
        kernel,
        out_shape=outs,
        in_specs=[SM if s else VM for s in smem],
        out_specs=jax.tree.map(lambda _: VM, outs),
        scratch_shapes=scratch,
        name=name,
        cost_estimate=cost,
        compiler_params=pltpu.CompilerParams(vmem_limit_bytes=mib * MIB),
    )(*ins)


def cost(scores, products):
    return pl.CostEstimate(
        flops=2 * 256 * scores * products, bytes_accessed=4 * scores, transcendentals=scores
    )


def dot(a, b):
    return jnp.dot(a, b, preferred_element_type=F32)


def dot_nt(a, b):
    return lax.dot_general(a, b, (((1,), (1,)), ((), ())), preferred_element_type=F32)


def softmax_t(scores):
    top = jnp.max(scores, axis=0, keepdims=True)
    e = jnp.exp2((scores - top) * (SCALE * math.log2(math.e)))
    return (e * (1.0 / jnp.sum(e, axis=0, keepdims=True))).astype(BF)


def head_columns(meta_ref, d, ref, base, p, W):
    at = base + meta_ref[1 + d] * 2 * W
    if W == HD:
        block = ref[:, pl.ds(pl.multiple_of(at, 128), 128)]
        return jnp.where(meta_ref[0] == 0, block[:, :HD], block[:, HD:])
    at = at + meta_ref[0] * W + (p // 2) * 128
    half = slice((p % 2) * HD, (p % 2 + 1) * HD)
    return ref[:, pl.ds(pl.multiple_of(at, 128), 128)][:, half]


def beside(a, b):
    return jnp.concatenate([a, b], axis=1)


def pack_own_kernel(meta_ref, x_ref, cq_ref, out_ref, *, p):
    C, R2, _ = out_ref.shape
    R, D = cq_ref.shape
    W = D // (2 * C)
    for d in range(C):
        cols = functools.partial(head_columns, meta_ref, d, p=p, W=W)
        out_ref[d, :R] = beside(cols(x_ref, D), cols(x_ref, 0))
        out_ref[d, R:] = beside(cols(x_ref, 2 * D), cols(cq_ref, 0))


def pack_sib_kernel(meta_ref, own_ref, go_ref, t_ref, xs_ref, cqs_ref, gos_ref, ts_ref, *msgs, p):
    C = len(msgs)
    R, D = go_ref.shape
    W = D // (2 * C)
    keep = meta_ref[2 + C] == 1
    for d in range(C):
        cols = functools.partial(head_columns, meta_ref, d, p=p, W=W)
        msg = msgs[d]
        msg[:R] = own_ref[d, :R]
        msg[R : 2 * R] = beside(cols(xs_ref, D), cols(xs_ref, 0))
        msg[2 * R : 3 * R] = own_ref[d, R:]
        msg[3 * R : 4 * R] = beside(cols(xs_ref, 2 * D), cols(cqs_ref, 0))
        msg[4 * R : 5 * R] = beside(cols(go_ref, 0), cols(gos_ref, 0))
        tk = jnp.where(keep, cols(t_ref, 0), cols(ts_ref, 0))
        tv = jnp.where(keep, cols(t_ref, D), cols(ts_ref, D))
        msg[5 * R :] = beside(tk, tv)


def pieces(refs):
    C = len(refs) // 2
    out = []
    for d in range(C):
        if d == 0:
            out.append(lambda rows, lanes, ref=refs[0]: ref[rows, lanes])
        else:
            lead = (0,) if len(refs[d].shape) == 3 else ()
            out.append(lambda rows, lanes, ref=refs[d], lead=lead: ref[(*lead, rows, lanes)])
        out.append(lambda rows, lanes, ref=refs[C + d]: ref[rows, lanes])
    return out


def put(msgs, block, rows, lanes, value):
    d, e = block // 2, block % 2
    if d == 0 or len(msgs[-1].shape) == 2:
        msgs[block][rows, lanes] = value
    else:
        msgs[d + 1][e, rows, lanes] = value


def message_shapes(C, rows, direct):
    if direct:
        return (sds((rows, 128)),) * (2 * C)
    return (sds((rows, 128)),) * 2 + (sds((2, rows, 128)),) * (C - 1)


def ahead(count, first, rest):
    value = first(0)
    for i in range(count):
        following = first(i + 1) if i + 1 < count else None
        rest(i, value)
        value = following


def layer_kernel(meta_ref, *refs, C, R, M):
    ins, outs = refs[:C], refs[C:-14]
    k_ref, v_ref, qT_ref, kT_ref, vT_ref, cqT_ref, goT_ref, agT_ref = refs[-14:-6]
    t_ref, dt_ref, oT_ref, back_ref, pT_ref, ds_ref = refs[-6:]
    L = 2 * C * R
    QB = 2 * R
    WB = min(512, L)
    MR = M // (2 * C)
    left, right = slice(0, HD), slice(HD, 2 * HD)
    for b in range(C):
        rows = slice(b * QB, (b + 1) * QB)
        k_ref[rows], v_ref[rows] = ins[b][:QB, left], ins[b][QB : 2 * QB, left]
        both = ins[b][:QB].T
        kT_ref[:, rows], qT_ref[:, rows] = both[left], both[right]
        both = ins[b][QB : 2 * QB].T
        vT_ref[:, rows], cqT_ref[:, rows] = both[left], both[right]
        both = ins[b][4 * R : 5 * R].T
        goT_ref[:, b * QB : b * QB + R], goT_ref[:, b * QB + R : (b + 1) * QB] = both[left], both[right]
    for d in range(C):

        @pl.when(meta_ref[1 + C] == d)
        def _():
            t_ref[...] = ins[d][5 * R :, :]

    tk, tv = t_ref[:, left], t_ref[:, right]
    tT = t_ref[...].T
    tkT, tvT = tT[left], tT[right]
    k, v, kT, vT = k_ref[...], v_ref[...], kT_ref[...], vT_ref[...]

    def block(b):
        return slice(b * WB, (b + 1) * WB)

    def attend(b, scores):
        p = softmax_t(scores)
        pT_ref[:, block(b)] = p
        oT_ref[:, block(b)] = dot(vT, p)

    ahead(L // WB, lambda b: dot(k, qT_ref[:, block(b)]), attend)
    dtk = dtv = None
    h = R // 2

    def mingle(b, products):
        nonlocal dtk, dtv
        cols = block(b)
        scores, xT, att, dp = products
        goT = goT_ref[:, cols]
        wide = goT.astype(F32)
        cp = softmax_t(scores)
        mix = dot(tvT, cp)
        back_ref[right, cols] = (att + mix).astype(BF)
        delta = jnp.sum(wide * mix, axis=0, keepdims=True)
        ds = (cp.astype(F32) * (dp - delta)).astype(BF)
        dq = dot(tkT, ds) * SCALE
        agT_ref[:, cols] = (wide + dq).astype(BF)
        dcq = dq.astype(BF)
        x, y = dot_nt(ds, xT), dot_nt(cp, goT)
        dtk, dtv = (x, y) if dtk is None else (dtk + x, dtv + y)
        for i in range(WB // R):
            at = i * R
            halves = jnp.concatenate([dcq[:, at : at + h], dcq[:, at + h : at + R]], axis=0)
            put(outs, b * (WB // R) + i, slice(2 * R, 2 * R + h), slice(None), halves.T)

    def scores_of(b):
        att = oT_ref[:, block(b)].astype(BF).astype(F32)
        xT = (att + cqT_ref[:, block(b)].astype(F32)).astype(BF)
        return dot(tk, xT), xT, att, dot(tv, goT_ref[:, block(b)])

    ahead(L // WB, scores_of, mingle)
    dt_ref[...] = beside(dtk * SCALE, dtv).astype(BF)
    for i in range(2 * C):
        start = pl.multiple_of(meta_ref[3 + C + i] * MR, MR)
        put(outs, i, slice(2 * R + h, None), slice(None), dt_ref[pl.ds(start, MR), :])
    agT = agT_ref[...]
    delta = jnp.sum(agT.astype(F32) * oT_ref[...], axis=0, keepdims=True)

    def back(b, dp):
        ds = (pT_ref[:, block(b)].astype(F32) * (dp - delta[:, block(b)])).astype(BF)
        ds_ref[:, block(b)] = ds
        back_ref[left, block(b)] = (dot(kT, ds) * SCALE).astype(BF)
        n = WB // R
        for i in range(n * b, n * b + n):
            put(outs, i, slice(0, R), slice(None), back_ref[:, i * R : (i + 1) * R].T)

    ahead(L // WB, lambda b: dot(v, agT_ref[:, block(b)]), back)
    dk = dot(ds_ref[...], qT_ref[...].T) * SCALE
    dv = dot(pT_ref[...], agT.T)
    both = beside(dk.astype(BF), dv.astype(BF))
    for i in range(2 * C):
        put(outs, i, slice(R, 2 * R), slice(None), both[i * R : (i + 1) * R])


def layer(meta, msgs, C, R, M, direct):
    L, H = 2 * C * R, HD
    return call(
        functools.partial(layer_kernel, C=C, R=R, M=M),
        "layer",
        [meta, *msgs],
        message_shapes(C, 2 * R + R // 2 + M // (2 * C), direct),
        LIMIT,
        [pltpu.VMEM((L, H), BF)] * 2
        + [pltpu.VMEM((H, L), BF)] * 6
        + [pltpu.VMEM((M, 128), BF)] * 2
        + [pltpu.VMEM((H, L), F32), pltpu.VMEM((128, L), BF)]
        + [pltpu.VMEM((L, L), BF)] * 2,
        cost(L * L + L * M, 6),
    )


def unpack_kernel(meta_ref, *refs, C, H):
    passes = [pieces(refs[2 * C * p : 2 * C * (p + 1)]) for p in range(H)]
    outs, (qkv_ref, comb_ref, dcq_ref, dt_ref) = refs[2 * C * H :][:4], refs[2 * C * H :][4:8]
    sems = refs[-1]
    R, D = comb_ref.shape
    W = D // (2 * C)
    side = meta_ref[0]
    left, right = slice(0, HD), slice(HD, 2 * HD)
    first, second = slice(0, R), slice(R, 2 * R)
    low, high, end = (
        slice(2 * R, 2 * R + R // 2),
        slice(2 * R, 2 * R + R // 2),
        slice(2 * R + R // 2, None),
    )

    def dcq(piece):
        return jnp.concatenate([piece(low, left), piece(high, right)], axis=0)

    parts = [
        (qkv_ref, 0, lambda piece: piece(first, left)),
        (qkv_ref, D, lambda piece: piece(second, left)),
        (qkv_ref, 2 * D, lambda piece: piece(second, right)),
        (comb_ref, 0, lambda piece: piece(first, right)),
        (dcq_ref, 0, dcq),
        (dt_ref, 0, lambda piece: piece(end, left)),
        (dt_ref, D, lambda piece: piece(end, right)),
    ]
    copies = []
    for n, (ref, base, read) in enumerate(parts):
        for d in range(C):
            at = base + meta_ref[1 + d] * 2 * W
            if H == 1:
                a, b = read(passes[0][2 * d]), read(passes[0][2 * d + 1])
                pair = beside(jnp.where(side == 0, a, b), jnp.where(side == 0, b, a))
                ref[:, pl.ds(pl.multiple_of(at, 128), 128)] = pair
                continue
            for e in range(2):
                core = side if e == 0 else 1 - side
                for p in range(0, H, 2):
                    pair = beside(read(passes[p][2 * d + e]), read(passes[p + 1][2 * d + e]))
                    start = pl.multiple_of(at + core * W + p * HD, 128)
                    ref[:, pl.ds(start, 128)] = pair
        target = outs[(0, 0, 0, 1, 2, 3, 3)[n]]
        cols = slice(base, base + D)
        copies.append(pltpu.make_async_copy(ref.at[:, cols], target.at[:, cols], sems.at[n]))
        copies[-1].start()
    for copy in copies:
        copy.wait()


def body(self_qkv, cross_query, thermal_kv, owners, grad_out):
    S, Hd = lax.axis_size("seq"), lax.axis_size("head")
    X = S // 2
    C = X * Hd
    R, D = cross_query.shape[1:]
    W = D // (2 * C)
    M = thermal_kv.shape[2]
    MR = M // (2 * C)
    offsets = [(i, j) for j in range(Hd) for i in range(X)]
    s, h = lax.axis_index("seq"), lax.axis_index("head")
    side, x = s % 2, s // 2
    owner_s, owner_h = owners[0] // Hd, owners[0] % Hd
    away = (x - owner_s // 2 + X) % X + X * ((h - owner_h + Hd) % Hd)
    keep = (owner_s % 2 == side).astype(jnp.int32)
    chips = [((x + i) % X) * Hd + (h + j) % Hd for i, j in offsets]
    ids = []
    for i, j in offsets:
        for e in (0, 1):
            ids.append((((x - i + X) % X) * 2 + (side if e == 0 else 1 - side)) * Hd + (h - j + Hd) % Hd)
    meta = jnp.stack([side, *chips, away, keep, *ids]).astype(jnp.int32)

    def to_sibling(a):
        return lax.ppermute(a, "seq", [(i, i ^ 1) for i in range(S)])

    def to_chip(a, d, sign, other=0):
        i, j = offsets[d]
        pairs = []
        for p in range(S):
            for q in range(Hd):
                there = ((p // 2 + sign * i) % X) * 2 + (p % 2 ^ other)
                pairs.append((p * Hd + q, there * Hd + (q + sign * j) % Hd))
        return lax.ppermute(a, GROUP, pairs)

    def after(arrays, *gates):
        return lax.optimization_barrier((list(arrays), gates))[0]

    bind = functools.partial
    H = W // HD
    own = (self_qkv[0], cross_query[0], grad_out[0], thermal_kv[0, 0])
    xs, cqs, gos, ts = [to_sibling(a) for a in own]
    x, cq, go, t = own
    msgs, got = [], []
    for p in range(H):
        if p:
            x, cq = after([x, cq], *msgs[p - 1])
        half = call(
            bind(pack_own_kernel, p=p), f"pack_own_{p}", [meta, x, cq], sds((C, 2 * R, 128)), 8
        )
        msgs.append(
            call(
                bind(pack_sib_kernel, p=p),
                f"pack_sib_{p}",
                [meta, half, go, t, xs, cqs, gos, ts],
                (sds((5 * R + M, 128)),) * C,
                12,
            )
        )
        got.append([to_chip(msgs[p][d], d, 1) for d in range(1, C)])
        if p:
            got[p - 1] = after(got[p - 1], *msgs[p])
    backs, outs = [], []
    for p in range(H):
        out = layer(meta, [msgs[p][0], *got[p]], C, R, M, p == H - 1)
        outs.append(out)
        if p + 1 < H:
            got[p + 1] = after(got[p + 1], *out)
        if p + 1 < H:
            backs.append([to_chip(out[d + 1], d, -1) for d in range(1, C)])
    pieces_in = []
    for p in range(H - 1):
        handed, *back = after([outs[p][1], *backs[p]], outs[p + 1][0])
        relayed = [to_sibling(handed)] + [to_sibling(g[1]) for g in back]
        pieces_in += [outs[p][0], *back, *relayed]
    out = outs[-1]
    straight = [to_chip(out[2 * d], d, -1) for d in range(1, C)]
    across = [to_chip(out[2 * d + 1], d, -1, 1) for d in range(C)]
    pieces_in += [out[0], *straight, *across]
    shapes = (sds((R, 3 * D)), sds((R, D)), sds((R, D)), sds((MR, 2 * D)))
    grad_qkv, combined, grad_cross, grad_thermal = pl.pallas_call(
        bind(unpack_kernel, C=C, H=H),
        out_shape=shapes,
        in_specs=[SM] + [VM] * len(pieces_in),
        out_specs=(pl.BlockSpec(memory_space=pltpu.HBM),) * 4,
        scratch_shapes=[pltpu.VMEM(o.shape, BF) for o in shapes] + [pltpu.SemaphoreType.DMA((7,))],
        name="unpack",
        compiler_params=pltpu.CompilerParams(vmem_limit_bytes=8 * MIB),
    )(meta, *pieces_in)
    return (combined[None], grad_qkv[None], grad_cross[None], grad_thermal[None])


def solution(mesh):
    rows = P("img", GROUP, None)
    return jax.shard_map(
        body,
        mesh=mesh,
        in_specs=(rows, rows, P("img", GROUP, None, None), P("img"), rows),
        out_specs=(rows, rows, rows, rows),
        check_vma=False,
    )
```

```python
import functools
import math

import jax
import jax.numpy as jnp
from jax import lax
from jax.experimental import pallas as pl
from jax.experimental.pallas import tpu as pltpu
from jax.sharding import PartitionSpec as P

BF = jnp.bfloat16
F32 = jnp.float32
HD = 64
GROUP = ("seq", "head")
VM = pl.BlockSpec(memory_space=pltpu.VMEM)
SM = pl.BlockSpec(memory_space=pltpu.SMEM)
SCALE = 1.0 / math.sqrt(HD)
MIB = 1 << 20
LIMIT = 36


def sds(shape, dtype=BF):
    return jax.ShapeDtypeStruct(shape, dtype)


def call(kernel, name, ins, outs, mib, scratch=(), cost=None):
    smem = [a.dtype == jnp.int32 for a in ins]
    return pl.pallas_call(
        kernel,
        out_shape=outs,
        in_specs=[SM if s else VM for s in smem],
        out_specs=jax.tree.map(lambda _: VM, outs),
        scratch_shapes=scratch,
        name=name,
        cost_estimate=cost,
        compiler_params=pltpu.CompilerParams(vmem_limit_bytes=mib * MIB),
    )(*ins)


def cost(scores, products):
    return pl.CostEstimate(
        flops=2 * 256 * scores * products, bytes_accessed=4 * scores, transcendentals=scores
    )


def dot(a, b):
    return jnp.dot(a, b, preferred_element_type=F32)


def dot_nt(a, b):
    return lax.dot_general(a, b, (((1,), (1,)), ((), ())), preferred_element_type=F32)


def softmax_t(scores):
    top = jnp.max(scores, axis=0, keepdims=True)
    e = jnp.exp2((scores - top) * (SCALE * math.log2(math.e)))
    return (e * (1.0 / jnp.sum(e, axis=0, keepdims=True))).astype(BF)


def head_columns(meta_ref, d, ref, base, p, W):
    at = base + meta_ref[1 + d] * 2 * W
    if W == HD:
        block = ref[:, pl.ds(pl.multiple_of(at, 128), 128)]
        return jnp.where(meta_ref[0] == 0, block[:, :HD], block[:, HD:])
    at = at + meta_ref[0] * W + (p // 2) * 128
    half = slice((p % 2) * HD, (p % 2 + 1) * HD)
    return ref[:, pl.ds(pl.multiple_of(at, 128), 128)][:, half]


def beside(a, b):
    return jnp.concatenate([a, b], axis=1)


def pack_own_kernel(meta_ref, x_ref, cq_ref, out_ref, *, p):
    C, R2, _ = out_ref.shape
    R, D = cq_ref.shape
    W = D // (2 * C)
    for d in range(C):
        cols = functools.partial(head_columns, meta_ref, d, p=p, W=W)
        out_ref[d, :R] = beside(cols(x_ref, D), cols(x_ref, 0))
        out_ref[d, R:] = beside(cols(x_ref, 2 * D), cols(cq_ref, 0))


def pack_sib_kernel(meta_ref, own_ref, go_ref, t_ref, xs_ref, cqs_ref, gos_ref, ts_ref, *msgs, p):
    C = len(msgs)
    R, D = go_ref.shape
    W = D // (2 * C)
    keep = meta_ref[2 + C] == 1
    for d in range(C):
        cols = functools.partial(head_columns, meta_ref, d, p=p, W=W)
        msg = msgs[d]
        msg[:R] = own_ref[d, :R]
        msg[R : 2 * R] = beside(cols(xs_ref, D), cols(xs_ref, 0))
        msg[2 * R : 3 * R] = own_ref[d, R:]
        msg[3 * R : 4 * R] = beside(cols(xs_ref, 2 * D), cols(cqs_ref, 0))
        msg[4 * R : 5 * R] = beside(cols(go_ref, 0), cols(gos_ref, 0))
        own = beside(cols(t_ref, 0), cols(t_ref, D))
        sib = beside(cols(ts_ref, 0), cols(ts_ref, D))
        msg[5 * R :] = jnp.where(keep, own, sib)


def pieces(refs):
    C = len(refs) // 2
    out = []
    for d in range(C):
        if d == 0:
            out.append(lambda rows, lanes, ref=refs[0]: ref[rows, lanes])
        else:
            lead = (0,) if len(refs[d].shape) == 3 else ()
            out.append(lambda rows, lanes, ref=refs[d], lead=lead: ref[(*lead, rows, lanes)])
        out.append(lambda rows, lanes, ref=refs[C + d]: ref[rows, lanes])
    return out


def put(msgs, block, rows, lanes, value):
    d, e = block // 2, block % 2
    if d == 0 or len(msgs[-1].shape) == 2:
        msgs[block][rows, lanes] = value
    else:
        msgs[d + 1][e, rows, lanes] = value


def message_shapes(C, rows, direct):
    if direct:
        return (sds((rows, 128)),) * (2 * C)
    return (sds((rows, 128)),) * 2 + (sds((2, rows, 128)),) * (C - 1)


def ahead(count, first, rest):
    value = first(0)
    for i in range(count):
        following = first(i + 1) if i + 1 < count else None
        rest(i, value)
        value = following


def layer_kernel(meta_ref, *refs, C, R, M):
    ins, outs = refs[:C], refs[C:-14]
    k_ref, v_ref, qT_ref, kT_ref, vT_ref, cqT_ref, goT_ref, agT_ref = refs[-14:-6]
    t_ref, dt_ref, oT_ref, back_ref, pT_ref, ds_ref = refs[-6:]
    L = 2 * C * R
    QB = 2 * R
    WB = min(512, L)
    MR = M // (2 * C)
    left, right = slice(0, HD), slice(HD, 2 * HD)
    for b in range(C):
        rows = slice(b * QB, (b + 1) * QB)
        k_ref[rows], v_ref[rows] = ins[b][:QB, left], ins[b][QB : 2 * QB, left]
        both = ins[b][:QB].T
        kT_ref[:, rows], qT_ref[:, rows] = both[left], both[right]
        both = ins[b][QB : 2 * QB].T
        vT_ref[:, rows], cqT_ref[:, rows] = both[left], both[right]
        both = ins[b][4 * R : 5 * R].T
        goT_ref[:, b * QB : b * QB + R], goT_ref[:, b * QB + R : (b + 1) * QB] = both[left], both[right]
    for d in range(C):

        @pl.when(meta_ref[1 + C] == d)
        def _():
            t_ref[...] = ins[d][5 * R :, :]

    tk, tv = t_ref[:, left], t_ref[:, right]
    tT = t_ref[...].T
    tkT, tvT = tT[left], tT[right]
    k, v, kT, vT = k_ref[...], v_ref[...], kT_ref[...], vT_ref[...]

    def block(b):
        return slice(b * WB, (b + 1) * WB)

    def attend(b, scores):
        p = softmax_t(scores)
        pT_ref[:, block(b)] = p
        oT_ref[:, block(b)] = dot(vT, p)

    dtk = dtv = None
    h = R // 2

    def mingle(b, products):
        nonlocal dtk, dtv
        cols = block(b)
        scores, xT, att, dp = products
        goT = goT_ref[:, cols]
        wide = goT.astype(F32)
        cp = softmax_t(scores)
        mix = dot(tvT, cp)
        back_ref[right, cols] = (att + mix).astype(BF)
        delta = jnp.sum(wide * mix, axis=0, keepdims=True)
        ds = (cp.astype(F32) * (dp - delta)).astype(BF)
        dq = dot(tkT, ds) * SCALE
        agT_ref[:, cols] = (wide + dq).astype(BF)
        dcq = dq.astype(BF)
        x, y = dot_nt(ds, xT), dot_nt(cp, goT)
        dtk, dtv = (x, y) if dtk is None else (dtk + x, dtv + y)
        for i in range(WB // R):
            at = i * R
            halves = jnp.concatenate([dcq[:, at : at + h], dcq[:, at + h : at + R]], axis=0)
            put(outs, b * (WB // R) + i, slice(2 * R, 2 * R + h), slice(None), halves.T)

    def scores_of(b):
        att = oT_ref[:, block(b)].astype(BF).astype(F32)
        xT = (att + cqT_ref[:, block(b)].astype(F32)).astype(BF)
        return dot(tk, xT), xT, att, dot(tv, goT_ref[:, block(b)])

    def back(b, dp):
        delta = jnp.sum(agT_ref[:, block(b)].astype(F32) * oT_ref[:, block(b)], axis=0, keepdims=True)
        ds = (pT_ref[:, block(b)].astype(F32) * (dp - delta)).astype(BF)
        ds_ref[:, block(b)] = ds
        back_ref[left, block(b)] = (dot(kT, ds) * SCALE).astype(BF)
        n = WB // R
        for i in range(n * b, n * b + n):
            put(outs, i, slice(0, R), slice(None), back_ref[:, i * R : (i + 1) * R].T)

    stages = [
        lambda b, _: dot(k, qT_ref[:, block(b)]),
        attend,
        lambda b, _: scores_of(b),
        mingle,
        lambda b, _: dot(v, agT_ref[:, block(b)]),
        back,
    ]
    n = L // WB
    values = [None] * n
    for stage in range(len(stages)):
        for b in range(n):
            values[b] = stages[stage](b, values[b])
    dt_ref[...] = beside(dtk * SCALE, dtv).astype(BF)
    for i in range(2 * C):
        start = pl.multiple_of(meta_ref[3 + C + i] * MR, MR)
        put(outs, i, slice(2 * R + h, None), slice(None), dt_ref[pl.ds(start, MR), :])
    agT = agT_ref[...]
    dk = dot(ds_ref[...], qT_ref[...].T) * SCALE
    dv = dot(pT_ref[...], agT.T)
    both = beside(dk.astype(BF), dv.astype(BF))
    for i in range(2 * C):
        put(outs, i, slice(R, 2 * R), slice(None), both[i * R : (i + 1) * R])


def layer(meta, msgs, C, R, M, direct):
    L, H = 2 * C * R, HD
    return call(
        functools.partial(layer_kernel, C=C, R=R, M=M),
        "layer",
        [meta, *msgs],
        message_shapes(C, 2 * R + R // 2 + M // (2 * C), direct),
        LIMIT,
        [pltpu.VMEM((L, H), BF)] * 2
        + [pltpu.VMEM((H, L), BF)] * 6
        + [pltpu.VMEM((M, 128), BF)] * 2
        + [pltpu.VMEM((H, L), F32), pltpu.VMEM((128, L), BF)]
        + [pltpu.VMEM((L, L), BF)] * 2,
        cost(L * L + L * M, 6),
    )


def unpack_kernel(meta_ref, *refs, C, H):
    passes = [pieces(refs[2 * C * p : 2 * C * (p + 1)]) for p in range(H)]
    outs, (qkv_ref, comb_ref, dcq_ref, dt_ref) = refs[2 * C * H :][:4], refs[2 * C * H :][4:8]
    sems = refs[-1]
    R, D = comb_ref.shape
    W = D // (2 * C)
    side = meta_ref[0]
    left, right = slice(0, HD), slice(HD, 2 * HD)
    first, second = slice(0, R), slice(R, 2 * R)
    low, high, end = (
        slice(2 * R, 2 * R + R // 2),
        slice(2 * R, 2 * R + R // 2),
        slice(2 * R + R // 2, None),
    )

    def dcq(piece):
        return jnp.concatenate([piece(low, left), piece(high, right)], axis=0)

    parts = [
        (qkv_ref, 0, lambda piece: piece(first, left)),
        (qkv_ref, D, lambda piece: piece(second, left)),
        (qkv_ref, 2 * D, lambda piece: piece(second, right)),
        (comb_ref, 0, lambda piece: piece(first, right)),
        (dcq_ref, 0, dcq),
        (dt_ref, 0, lambda piece: piece(end, left)),
        (dt_ref, D, lambda piece: piece(end, right)),
    ]
    copies = []
    for n in (5, 6, 4, 3, 2, 1, 0):
        ref, base, read = parts[n]
        for d in range(C):
            at = base + meta_ref[1 + d] * 2 * W
            if H == 1:
                a, b = read(passes[0][2 * d]), read(passes[0][2 * d + 1])
                pair = beside(jnp.where(side == 0, a, b), jnp.where(side == 0, b, a))
                ref[:, pl.ds(pl.multiple_of(at, 128), 128)] = pair
                continue
            for e in range(2):
                core = side if e == 0 else 1 - side
                for p in range(0, H, 2):
                    pair = beside(read(passes[p][2 * d + e]), read(passes[p + 1][2 * d + e]))
                    start = pl.multiple_of(at + core * W + p * HD, 128)
                    ref[:, pl.ds(start, 128)] = pair
        target = outs[(0, 0, 0, 1, 2, 3, 3)[n]]
        cols = slice(base, base + D)
        copies.append(pltpu.make_async_copy(ref.at[:, cols], target.at[:, cols], sems.at[n]))
        copies[-1].start()
    for copy in copies:
        copy.wait()


def body(self_qkv, cross_query, thermal_kv, owners, grad_out):
    S, Hd = lax.axis_size("seq"), lax.axis_size("head")
    X = S // 2
    C = X * Hd
    R, D = cross_query.shape[1:]
    W = D // (2 * C)
    M = thermal_kv.shape[2]
    MR = M // (2 * C)
    offsets = [(i, j) for j in range(Hd) for i in range(X)]
    s, h = lax.axis_index("seq"), lax.axis_index("head")
    side, x = s % 2, s // 2
    owner_s, owner_h = owners[0] // Hd, owners[0] % Hd
    away = (x - owner_s // 2 + X) % X + X * ((h - owner_h + Hd) % Hd)
    keep = (owner_s % 2 == side).astype(jnp.int32)
    chips = [((x + i) % X) * Hd + (h + j) % Hd for i, j in offsets]
    ids = []
    for i, j in offsets:
        for e in (0, 1):
            ids.append((((x - i + X) % X) * 2 + (side if e == 0 else 1 - side)) * Hd + (h - j + Hd) % Hd)
    meta = jnp.stack([side, *chips, away, keep, *ids]).astype(jnp.int32)

    def to_sibling(a):
        return lax.ppermute(a, "seq", [(i, i ^ 1) for i in range(S)])

    def to_chip(a, d, sign, other=0):
        i, j = offsets[d]
        pairs = []
        for p in range(S):
            for q in range(Hd):
                there = ((p // 2 + sign * i) % X) * 2 + (p % 2 ^ other)
                pairs.append((p * Hd + q, there * Hd + (q + sign * j) % Hd))
        return lax.ppermute(a, GROUP, pairs)

    def after(arrays, *gates):
        return lax.optimization_barrier((list(arrays), gates))[0]

    bind = functools.partial
    H = W // HD
    own = (self_qkv[0], cross_query[0], grad_out[0], thermal_kv[0, 0])
    xs, cqs, gos, ts = [to_sibling(a) for a in own]
    x, cq, go, t = own
    msgs, got = [], []
    for p in range(H):
        if p:
            x, cq = after([x, cq], *msgs[p - 1])
        half = call(
            bind(pack_own_kernel, p=p), f"pack_own_{p}", [meta, x, cq], sds((C, 2 * R, 128)), 8
        )
        msgs.append(
            call(
                bind(pack_sib_kernel, p=p),
                f"pack_sib_{p}",
                [meta, half, go, t, xs, cqs, gos, ts],
                (sds((5 * R + M, 128)),) * C,
                12,
            )
        )
        got.append([to_chip(msgs[p][d], d, 1) for d in range(1, C)])
        if p:
            got[p - 1] = after(got[p - 1], *msgs[p])
    backs, outs = [], []
    for p in range(H):
        out = layer(meta, [msgs[p][0], *got[p]], C, R, M, p == H - 1)
        outs.append(out)
        if p + 1 < H:
            got[p + 1] = after(got[p + 1], *out)
        if p + 1 < H:
            backs.append([to_chip(out[d + 1], d, -1) for d in range(1, C)])
    pieces_in = []
    for p in range(H - 1):
        handed, *back = after([outs[p][1], *backs[p]], outs[p + 1][0])
        relayed = [to_sibling(handed)] + [to_sibling(g[1]) for g in back]
        pieces_in += [outs[p][0], *back, *relayed]
    out = outs[-1]
    straight = [to_chip(out[2 * d], d, -1) for d in range(1, C)]
    across = [to_chip(out[2 * d + 1], d, -1, 1) for d in range(C)]
    pieces_in += [out[0], *straight, *across]
    shapes = (sds((R, 3 * D)), sds((R, D)), sds((R, D)), sds((MR, 2 * D)))
    grad_qkv, combined, grad_cross, grad_thermal = pl.pallas_call(
        bind(unpack_kernel, C=C, H=H),
        out_shape=shapes,
        in_specs=[SM] + [VM] * len(pieces_in),
        out_specs=(pl.BlockSpec(memory_space=pltpu.HBM),) * 4,
        scratch_shapes=[pltpu.VMEM(o.shape, BF) for o in shapes] + [pltpu.SemaphoreType.DMA((7,))],
        name="unpack",
        compiler_params=pltpu.CompilerParams(vmem_limit_bytes=8 * MIB),
    )(meta, *pieces_in)
    return (combined[None], grad_qkv[None], grad_cross[None], grad_thermal[None])


def solution(mesh):
    rows = P("img", GROUP, None)
    return jax.shard_map(
        body,
        mesh=mesh,
        in_specs=(rows, rows, P("img", GROUP, None, None), P("img"), rows),
        out_specs=(rows, rows, rows, rows),
        check_vma=False,
    )
```
